512 devices in a mesh: gx: 16 (over z), gz: 8 (over y_lo, x), pa: 4 (over y_hi, core).
Axes of the slice: x: 4, y: 4 (y_hi: 2, y_lo: 2; y = y_hi * 2 + y_lo), z: 16, core: 2. Of those that a mesh axis runs over, the one named last changes fastest.
Arguments:
- velocity: float32 [8, 128, 128, 512], P('pa', 'gx', 'gz'), may hold values from 0.7 to 2.3
- wave_now: float32 [8, 128, 128, 512], P('pa', 'gx', 'gz'), may hold values from -6 to 6
- wave_prev: float32 [8, 128, 128, 512], P('pa', 'gx', 'gz'), may hold values from -6 to 6
- observed: float32 [128, 128, 512], P('gx', 'gz'), may hold values from -6 to 6
- receiver: int32 [128, 128, 512], P('gx', 'gz'), may hold values 0 or 1
- spread: int32 [2], replicated, may hold values from 100 to 10000, as said below
Outputs:
- update: float32 [8, 128, 128, 512], P('pa', 'gx', 'gz')
The draws below stay inside these ranges and needn't reach their ends.
Inputs may be any that keep to these rules, and one draw needn't show every extreme that they name: spread[0] is the numerator, 100 to 200, and spread[1] the denominator, 10000.
All inputs are finite; a program needn't handle non-finite values. No bound on the sum of `receiver` on one device may be relied on, other than what follows from the above.
Results may differ from the reference program's by a relative error of at most 0.0003.
Values sent between devices are 32-bit elements; how exact they have to be, the bound alone decides.
A program may use at most 64 MiB of HBM per device.

```python
import math
import jax
import jax.numpy as jnp
from jax import lax

NY = 512
STEPS = 4
P_SIZE = 8
NX = 128
NZ = 128


def draw_velocity(key, part):
    key_base, key_rank, key_rough, key_fluct = jax.random.split(jax.random.fold_in(key, 11), 4)
    background = jax.random.uniform(key_base, (NX, NZ, NY), jnp.float32, 1.3, 1.7)
    ranking = jax.random.permutation(key_rank, P_SIZE).astype(jnp.float32)
    amplitude = 0.02 * jnp.exp(math.log(10.0) * ranking / max(P_SIZE - 1, 1))
    roughness = jnp.exp(jax.random.uniform(key_rough, (NX, NZ, NY), jnp.float32, math.log(0.3), math.log(3.0)))
    x_ramp = (1.0 + 2.0 * jnp.arange(NX, dtype=jnp.float32) / NX) / 3.0
    envelope = roughness * x_ramp[:, None, None]
    fluctuation = jax.random.uniform(key_fluct, (P_SIZE, NX, NZ, NY), jnp.float32, -1.0, 1.0)
    return background[None] + amplitude[:, None, None, None] * envelope[None] * fluctuation


def draw_spread(key, part):
    key_top = jax.random.fold_in(key, 23)
    numerator = jax.random.randint(key_top, (1,), 100, 201)
    denominator = numerator * 0 + 10000
    return jnp.concatenate([numerator, denominator]).astype(jnp.int32)


def touch_ends(values, own_key, smallest, high):
    spot = [jax.random.randint(jax.random.fold_in(own_key, axis), (), 0, length) for axis, length in enumerate(values.shape)]
    widest = values.shape.index(max(values.shape))
    neighbour = spot[:widest] + [(spot[widest] + 1) % values.shape[widest]] + spot[widest + 1:]
    return values.at[tuple(spot)].set(smallest).at[tuple(neighbour)].set(high)


def shard_levels(key, shape, pieces, least, top_value):
    def one(axis_at, shards_of):
        steps = jax.random.uniform(jax.random.fold_in(jax.random.fold_in(key, 6), axis_at), (shards_of,), jnp.float32, least / len(pieces), top_value / len(pieces))
        return jnp.repeat(jnp.exp(steps), shape[axis_at] // shards_of).reshape((-1,) + (1,) * (len(shape) - axis_at - 1))

    factor_of = one(*pieces[0])
    for cut in pieces[1:]:
        factor_of = factor_of * one(*cut)
    return factor_of


def scatter_about(key, extent, scale, reach, cuts=(), kind=jnp.bfloat16):
    array = scale * jax.random.normal(key, extent, jnp.float32)
    if cuts:
        array = array * shard_levels(key, extent, cuts, -0.22, 0.18)
    return jnp.clip(array, -reach, reach).astype(kind)


def setup_inputs(seed: int = 0) -> dict:
    key_list = jax.random.split(jax.random.key(seed), 7)
    return {
        "velocity": draw_velocity(jax.random.fold_in(key_list[6], 71), 0),
        "wave_now": scatter_about(key_list[1], (P_SIZE, NX, NZ, NY), 1.0, 6.0, ((0, 4), (1, 16), (2, 8)), jnp.float32),
        "wave_prev": scatter_about(key_list[2], (P_SIZE, NX, NZ, NY), 1.0, 6.0, ((0, 4), (1, 16), (2, 8)), jnp.float32),
        "observed": scatter_about(key_list[3], (NX, NZ, NY), 1.0, 6.0, ((0, 16), (1, 8)), jnp.float32),
        "receiver": touch_ends((jax.random.randint(key_list[4], (NX, NZ, NY), 0, 2) < 1).astype(jnp.int32), jax.random.fold_in(key_list[4], 1), 0, 1),
        "spread": draw_spread(jax.random.fold_in(key_list[6], 71), 0),
    }


courant = 0.045
centre_coef = -7.5
near_coef = 4.0 / 3.0
far_coef = -1.0 / 12.0

def shifted(padded, which_dim, offset, dims):
    starts = [2, 2, 2]
    starts[which_dim] += offset
    limits = [starts[k] + dims[k] for k in range(3)]
    return lax.slice(padded, starts, limits)

def laplace(wave_field):
    dims = wave_field.shape
    padded = jnp.pad(wave_field, 2)
    summed = centre_coef * wave_field
    for which_dim in range(3):
        summed = summed + near_coef * (shifted(padded, which_dim, -1, dims) + shifted(padded, which_dim, 1, dims))
        summed = summed + far_coef * (shifted(padded, which_dim, -2, dims) + shifted(padded, which_dim, 2, dims))
    return summed

def misfit(velocity_one, current, previous, observed, receiver_mask):
    coefficient = courant * velocity_one * velocity_one
    for step_index in range(STEPS):
        following = 2.0 * current - previous + coefficient * laplace(current)
        previous, current = (current, following)
    difference = current - observed
    return 0.5 * jnp.sum(receiver_mask * difference * difference)

def reference(velocity, wave_now, wave_prev, observed, receiver, spread):
    receiver_mask = receiver.astype(jnp.float32)

    def one_gradient(packed):
        return jax.grad(misfit)(packed[0], packed[1], packed[2], observed, receiver_mask)
    gradient = lax.map(one_gradient, (velocity, wave_now, wave_prev))
    width_scale = spread[0].astype(jnp.float32) / spread[1].astype(jnp.float32)

    def distance_row(velocity_row):
        differences = velocity_row[None] - velocity
        return lax.optimization_barrier(jnp.mean(differences * differences, axis=(1, 2, 3)))
    distance = lax.map(distance_row, velocity)
    weight = jnp.exp(-distance / width_scale)
    count = velocity.shape[0]

    def update_row(packed):
        weight_row, velocity_row = packed
        contrib = -gradient + 2.0 / width_scale * (velocity_row[None] - velocity)
        return lax.optimization_barrier(jnp.sum(weight_row[:, None, None, None] * contrib, axis=0)) / count
    return lax.map(update_row, (weight, velocity))
```

```python
import functools

import jax
import jax.numpy as jnp
from jax import lax
from jax.experimental import pallas as pl
from jax.experimental.pallas import tpu as pltpu
from jax.sharding import PartitionSpec as P


STEPS = 4
courant = 0.045
centre_coef = -7.5
near_coef = 4.0 / 3.0
far_coef = -1.0 / 12.0
middle = 1.5
ZC = 8
MESH = pl.DeviceIdType.MESH


def kernel(
    GX, GZ, PA, cells, NX, NZ,
    spread, vel_hbm, now_hbm, prev_hbm, obs_hbm, rec_hbm, out_hbm,
    natural, natural_obs, natural_rec, natural_out,
    U, V, C, W0, L, LAM, S, OB, MK,
    RV, AR, CUR, H, HR,
    in_sem, out_sem, halo_send, halo_recv, vel_send, vel_recv, ar_send, ar_recv,
    h_send, h_recv,
):
    gx, gz, pa = lax.axis_index("gx"), lax.axis_index("gz"), lax.axis_index("pa")
    core, hi = lax.rem(pa, 2), pa // 2
    partner = hi * 2 + (1 - core)
    across = (1 - hi) * 2 + core
    diagonal = (1 - hi) * 2 + (1 - core)

    loads = [
        pltpu.make_async_copy(now_hbm, natural.at[0], in_sem.at[0]),
        pltpu.make_async_copy(vel_hbm, natural.at[1], in_sem.at[1]),
        pltpu.make_async_copy(prev_hbm, natural.at[2], in_sem.at[2]),
        pltpu.make_async_copy(obs_hbm, natural_obs, in_sem.at[3]),
        pltpu.make_async_copy(rec_hbm, natural_rec, in_sem.at[4]),
    ]
    for load in loads:
        load.start()

    def turn(index, group, stride, step):
        low = lax.rem(index, stride)
        digit = lax.rem(index // stride, group)
        high = index // (stride * group)
        return (high * group + lax.rem(digit + step, group)) * stride + low

    stages = [
        [{"gx": turn(gx, 4, 1, j)} for j in (1, 2, 3)],
        [{"gx": turn(gx, GX // 4, 4, j)} for j in range(1, GX // 4)],
        [{"gz": turn(gz, 4, 1, j)} for j in (1, 2, 3)],
        [{"gz": turn(gz, GZ // 4, 4, j)} for j in range(1, GZ // 4)],
        [{"pa": turn(pa, 4, 1, j)} for j in (1, 2, 3)],
    ]
    halo_dest = [
        {"gx": lax.rem(gx + GX - 1, GX)},
        {"gx": lax.rem(gx + 1, GX)},
        {"gz": lax.rem(gz + GZ - 1, GZ)},
        {"gz": lax.rem(gz + 1, GZ)},
    ]
    sends_halo = [gx > 0, gx < GX - 1, gz > 0, gz < GZ - 1]
    gets_halo = [gx < GX - 1, gx > 0, gz < GZ - 1, gz > 0]

    barrier = pltpu.get_barrier_semaphore()
    for d in range(4):
        @pl.when(sends_halo[d])
        def _(d=d):
            pl.semaphore_signal(barrier, inc=1, device_id=halo_dest[d], device_id_type=MESH)
    count = 0
    for stage in stages:
        for peer in stage:
            pl.semaphore_signal(barrier, inc=1, device_id=peer, device_id_type=MESH)
            count += 1

    zero_x = jnp.zeros((2, NZ, 8, 128), jnp.float32)
    zero_z = jnp.zeros((NX, 2, 8, 128), jnp.float32)

    @pl.when(gx == 0)
    def _():
        for n in range(7):
            U[n, 0:2, 2 : NZ + 2] = zero_x

    @pl.when(gx == GX - 1)
    def _():
        for n in range(7):
            U[n, NX + 2 : NX + 4, 2 : NZ + 2] = zero_x

    @pl.when(gz == 0)
    def _():
        for n in range(7):
            U[n, 2 : NX + 2, 0:2] = zero_z

    @pl.when(gz == GZ - 1)
    def _():
        for n in range(7):
            U[n, 2 : NX + 2, NZ + 2 : NZ + 4] = zero_z

    def to_tiles(read, write):
        def plane(x, carry):
            for zt in range(NZ // 8):
                parts = [read(k, x, zt) for k in range(8)]
                write(x, zt * 8, jnp.swapaxes(jnp.stack(parts, axis=0), 0, 1))
            return carry
        lax.fori_loop(0, NX, plane, 0)

    def read_wave(slot):
        def read(k, x, zt):
            y = (k % 4) * 128
            return natural[slot, k // 4, x, zt * 8 : zt * 8 + 8, y : y + 128]
        return read

    def read_plain(ref):
        def read(k, x, zt):
            y = (k % 4) * 128
            return ref[x, zt * 8 : zt * 8 + 8, y : y + 128].astype(jnp.float32)
        return read

    def write_now(x, z, tiles):
        U[0, x + 2, z + 2 : z + 10] = tiles

    def write_velocity(x, z, tiles):
        V[x, z : z + 8] = tiles
        C[x, z : z + 8] = courant * tiles * tiles

    def write_prev(x, z, tiles):
        W0[x, z : z + 8] = tiles

    def write_obs(x, z, tiles):
        OB[x, z : z + 8] = tiles

    def write_mask(x, z, tiles):
        MK[x, z : z + 8] = tiles

    def halo(n, d):
        field = U.at[n]
        inner_x, inner_z = pl.ds(2, NX), pl.ds(2, NZ)
        source, target = [
            ((pl.ds(2, 2), inner_z), (pl.ds(NX + 2, 2), inner_z)),
            ((pl.ds(NX, 2), inner_z), (pl.ds(0, 2), inner_z)),
            ((inner_x, pl.ds(2, 2)), (inner_x, pl.ds(NZ + 2, 2))),
            ((inner_x, pl.ds(NZ, 2)), (inner_x, pl.ds(0, 2))),
        ][d]
        return pltpu.make_async_remote_copy(
            src_ref=field.at[source],
            dst_ref=field.at[target],
            send_sem=halo_send.at[n, d],
            recv_sem=halo_recv.at[n, d],
            device_id=halo_dest[d],
            device_id_type=MESH,
        )

    def send_halo(n, d):
        @pl.when(sends_halo[d])
        def _():
            halo(n, d).start()

    def wait_halo(n, d):
        @pl.when(gets_halo[d])
        def _():
            halo(n, d).wait_recv()

    loads[0].wait()
    to_tiles(read_wave(0), write_now)
    peers = count
    for gets in gets_halo:
        peers = peers + jnp.where(gets, 1, 0)
    pl.semaphore_wait(barrier, peers)
    for d in range(4):
        send_halo(0, d)

    loads[1].wait()
    to_tiles(read_wave(1), write_velocity)

    slab = NX // PA
    vel_copies = []
    for j in (1, 2, 3):
        q = lax.rem(pa + j, PA)
        vel_copies.append(
            pltpu.make_async_remote_copy(
                src_ref=V.at[pl.ds(q * slab, slab)],
                dst_ref=RV.at[j],
                send_sem=vel_send.at[j],
                recv_sem=vel_recv.at[j],
                device_id={"pa": q},
                device_id_type=MESH,
            )
        )
    for copy in vel_copies:
        copy.start()

    loads[2].wait()
    to_tiles(read_wave(2), write_prev)
    loads[3].wait()
    to_tiles(read_plain(natural_obs), write_obs)
    loads[4].wait()
    to_tiles(read_plain(natural_rec), write_mask)

    shape = (ZC, 8, 128)
    lane = lax.broadcasted_iota(jnp.int32, shape, 2)
    sub = lax.broadcasted_iota(jnp.int32, shape, 1)
    lane2 = lax.broadcasted_iota(jnp.int32, (8, 128), 1)
    sub2 = lax.broadcasted_iota(jnp.int32, (8, 128), 0)

    scale = (
        jnp.full((8, 128), spread[0], jnp.int32).astype(jnp.float32)
        / jnp.full((8, 128), spread[1], jnp.int32).astype(jnp.float32)
    )
    pull = 2.0 / scale

    def laplace(n, x, z):
        here = U[n, x + 2, pl.ds(z + 2, ZC)]
        near = U[n, x + 1, pl.ds(z + 2, ZC)] + U[n, x + 3, pl.ds(z + 2, ZC)]
        far = U[n, x, pl.ds(z + 2, ZC)] + U[n, x + 4, pl.ds(z + 2, ZC)]
        near = near + (U[n, x + 2, pl.ds(z + 1, ZC)] + U[n, x + 2, pl.ds(z + 3, ZC)])
        far = far + (U[n, x + 2, pl.ds(z, ZC)] + U[n, x + 2, pl.ds(z + 4, ZC)])
        before = pltpu.roll(here, 1, 1)
        before = jnp.where((sub == 0) | (sub == 4), 0.0, before)
        after = pltpu.roll(here, 7, 1)
        after = jnp.where((sub == 3) | (sub == 7), 0.0, after)
        near = near + (
            pltpu.roll(jnp.where(lane == 127, before, here), 1, 2)
            + pltpu.roll(jnp.where(lane == 0, after, here), 127, 2)
        )
        far = far + (
            pltpu.roll(jnp.where(lane >= 126, before, here), 2, 2)
            + pltpu.roll(jnp.where(lane <= 1, after, here), 126, 2)
        )
        return here, centre_coef * here + near_coef * near + far_coef * far

    def advance(n, x, z):
        here, applied = laplace(n, x, z)
        at = (x, pl.ds(z, ZC))
        inner = (x + 2, pl.ds(z + 2, ZC))
        if n < STEPS:
            older = W0[at] if n == 0 else U[(n - 1,) + inner]
            newer = 2.0 * here - older + C[at] * applied
            if n < STEPS - 1:
                L[(n,) + at] = applied
                U[(n + 1,) + inner] = newer
            else:
                adjoint = MK[at] * (newer - OB[at])
                S[at] = adjoint * applied
                LAM[(0,) + at] = adjoint
                U[(n + 1,) + inner] = C[at] * adjoint
        else:
            k = n - STEPS
            adjoint = 2.0 * LAM[(k,) + at] + applied
            if k > 0:
                adjoint = adjoint - LAM[(k - 1,) + at]
            total = S[at] + adjoint * L[(STEPS - 2 - k,) + at]
            if k < STEPS - 2:
                S[at] = total
                LAM[(k + 1,) + at] = adjoint
                U[(n + 1,) + inner] = C[at] * adjoint
            else:
                velocity = V[at]
                H[at] = (2.0 * courant) * velocity * total + pull[None] * (velocity - middle)

    def planes(n, first, count_x):
        per = NZ // ZC

        def body(i, carry):
            advance(n, first + i // per, lax.rem(i, per) * ZC)
            return carry
        lax.fori_loop(0, count_x * per, body, 0)

    def ar_copies(stage):
        return [
            pltpu.make_async_remote_copy(
                src_ref=CUR.at[stage],
                dst_ref=AR.at[stage, j],
                send_sem=ar_send.at[stage, j],
                recv_sem=ar_recv.at[stage, j],
                device_id=peer,
                device_id_type=MESH,
            )
            for j, peer in enumerate(stages[stage])
        ]

    def ar_start(stage):
        for copy in ar_copies(stage):
            copy.start()

    def ar_finish(stage):
        total = CUR[stage]
        for j, copy in enumerate(ar_copies(stage)):
            copy.wait_recv()
            total = total + AR[stage, j]
        CUR[stage + 1] = total

    def pair_sums():
        for copy in vel_copies:
            copy.wait_recv()

        def body(i, sums):
            x, z = i // NZ, lax.rem(i, NZ)
            tile = [V[pa * slab + x, z]] + [RV[j, x, z] for j in (1, 2, 3)]
            swapped = [pltpu.roll(t, 4, 0) for t in tile]
            out, at = [], 0
            for a in range(4):
                for b in range(a, 4):
                    if b > a:
                        delta = tile[a] - tile[b]
                        out.append(sums[at] + delta * delta)
                        at += 1
                    delta = tile[a] - swapped[b]
                    out.append(sums[at] + delta * delta)
                    at += 1
            return tuple(out)

        zero = jnp.zeros((8, 128), jnp.float32)
        sums = lax.fori_loop(0, slab * NZ, body, (zero,) * 16)
        groups = [lax.rem(pa + PA - j, PA) for j in range(4)]
        table, at = zero, 0
        for a in range(4):
            for b in range(a, 4):
                if b > a:
                    plain = jnp.sum(sums[at], axis=1, keepdims=True)
                    at += 1
                    spot = (lane2 == groups[a] * 8 + groups[b] * 2) | (lane2 == groups[b] * 8 + groups[a] * 2)
                    table = jnp.where(spot, plain, table)
                crossed = jnp.sum(sums[at], axis=1, keepdims=True)
                at += 1
                table = jnp.where(lane2 == groups[a] * 8 + groups[b] * 2 + 1, crossed, table)
                if b > a:
                    turned = pltpu.roll(jnp.broadcast_to(crossed, (8, 128)), 4, 0)
                    table = jnp.where(lane2 == groups[b] * 8 + groups[a] * 2 + 1, turned, table)
        CUR[0] = table

    def h_copy(kind, x, src, dest):
        return pltpu.make_async_remote_copy(
            src_ref=src,
            dst_ref=HR.at[kind, x],
            send_sem=h_send.at[kind, x],
            recv_sem=h_recv.at[kind, x],
            device_id={"pa": dest},
            device_id_type=MESH,
        )

    def h_own(x):
        return h_copy(0, x, H.at[x], partner)

    def h_across(x):
        return h_copy(1, x, H.at[x], across)

    def h_forward(x):
        return h_copy(2, x, HR.at[1, x], partner)

    for n in range(7):
        wait_halo(n, 2)
        wait_halo(n, 3)
        planes(n, 2, NX - 4)
        if n == 6:
            for x in range(2, NX - 2):
                h_across(x).start()
                h_own(x).start()
        wait_halo(n, 0)
        wait_halo(n, 1)
        planes(n, 0, 2)
        if n < 6:
            send_halo(n + 1, 0)
        else:
            for x in (0, 1):
                h_across(x).start()
                h_own(x).start()
        planes(n, NX - 2, 2)
        if n < 6:
            send_halo(n + 1, 1)
            send_halo(n + 1, 2)
            send_halo(n + 1, 3)
        else:
            for x in (NX - 2, NX - 1):
                h_across(x).start()
                h_own(x).start()
        if n == 1:
            pair_sums()
            ar_start(0)
        elif 2 <= n <= 5:
            ar_finish(n - 2)
            ar_start(n - 1)
    ar_finish(4)

    table = CUR[5]
    low = jnp.sum(jnp.where(sub2 < 4, table, 0.0), axis=0, keepdims=True)
    high = jnp.sum(jnp.where(sub2 < 4, 0.0, table), axis=0, keepdims=True)
    weight = jnp.exp(-(jnp.where(sub2 < 4, low, high) / cells) / scale)

    def column(index):
        picked = jnp.sum(jnp.where(lane2 == index, weight, 0.0), axis=1, keepdims=True)
        return jnp.broadcast_to(picked, (8, 128))

    groups = [pa, partner, across, diagonal]
    plain = [column(pa * 8 + g * 2) for g in groups]
    crossed = [column(pa * 8 + g * 2 + 1) for g in groups]
    all_weights = plain[0] + crossed[0]
    for g in (1, 2, 3):
        all_weights = all_weights + (plain[g] + crossed[g])
    count_all = 2 * PA
    own = pull * all_weights / count_all
    plain = [-w / count_all for w in plain]
    crossed = [-w / count_all for w in crossed]

    order = list(range(2, NX - 2)) + [0, 1, NX - 2, NX - 1]
    for x in order:
        h_across(x).wait_recv()
        h_forward(x).start()

    outs = []
    for at, x in enumerate(order):
        h_own(x).wait_recv()
        h_forward(x).wait_recv()
        for zt in range(NZ // 8):
            z = zt * 8
            result = own[None] * (V[x, z : z + 8] - middle)
            for g in range(4):
                tile = H[x, z : z + 8] if g == 0 else HR[g - 1, x, z : z + 8]
                result = result + plain[g][None] * tile + crossed[g][None] * pltpu.roll(tile, 4, 1)
            result = jnp.swapaxes(result, 0, 1)
            for k in range(8):
                y = (k % 4) * 128
                natural_out[k // 4, x, z : z + 8, y : y + 128] = result[k]
        copy = pltpu.make_async_copy(
            natural_out.at[:, pl.ds(x, 1)], out_hbm.at[:, pl.ds(x, 1)], out_sem.at[x]
        )
        copy.start()
        outs.append(copy)

    for n in range(7):
        for d in range(4):
            @pl.when(sends_halo[d])
            def _(n=n, d=d):
                halo(n, d).wait_send()
    for copy in vel_copies:
        copy.wait_send()
    for stage in range(5):
        for copy in ar_copies(stage):
            copy.wait_send()
    for x in order:
        h_across(x).wait_send()
        h_own(x).wait_send()
        h_forward(x).wait_send()
    for copy in outs:
        copy.wait()


def local(velocity, wave_now, wave_prev, observed, receiver, spread):
    GX, GZ, PA = lax.axis_size("gx"), lax.axis_size("gz"), lax.axis_size("pa")
    particles, NX, NZ, NY = velocity.shape
    cells = float(NX * GX * NZ * GZ * NY)
    any_space = pl.BlockSpec(memory_space=pl.ANY)
    tiles = (NX, NZ, 8, 128)
    f32 = jnp.float32
    dma = pltpu.SemaphoreType.DMA
    return pl.pallas_call(
        functools.partial(kernel, GX, GZ, PA, cells, NX, NZ),
        out_shape=jax.ShapeDtypeStruct(velocity.shape, f32),
        in_specs=[pl.BlockSpec(memory_space=pltpu.SMEM)] + [any_space] * 5,
        out_specs=any_space,
        scratch_shapes=[
            pltpu.VMEM((3,) + velocity.shape, f32),
            pltpu.VMEM(observed.shape, f32),
            pltpu.VMEM(receiver.shape, jnp.int32),
            pltpu.VMEM(velocity.shape, f32),
            pltpu.VMEM((7, NX + 4, NZ + 4, 8, 128), f32),
            pltpu.VMEM(tiles, f32),
            pltpu.VMEM(tiles, f32),
            pltpu.VMEM(tiles, f32),
            pltpu.VMEM((3,) + tiles, f32),
            pltpu.VMEM((3,) + tiles, f32),
            pltpu.VMEM(tiles, f32),
            pltpu.VMEM(tiles, f32),
            pltpu.VMEM(tiles, f32),
            pltpu.VMEM((4, NX // PA, NZ, 8, 128), f32),
            pltpu.VMEM((5, 3, 8, 128), f32),
            pltpu.VMEM((6, 8, 128), f32),
            pltpu.VMEM(tiles, f32),
            pltpu.VMEM((3,) + tiles, f32),
            dma((5,)),
            dma((NX,)),
            dma((7, 4)),
            dma((7, 4)),
            dma((4,)),
            dma((4,)),
            dma((5, 3)),
            dma((5, 3)),
            dma((3, NX)),
            dma((3, NX)),
        ],
        compiler_params=pltpu.CompilerParams(collective_id=0, has_side_effects=True),
    )(spread, velocity, wave_now, wave_prev, observed, receiver)


def solution(mesh):
    in_specs = (
        P("pa", "gx", "gz", None),
        P("pa", "gx", "gz", None),
        P("pa", "gx", "gz", None),
        P("gx", "gz", None),
        P("gx", "gz", None),
        P(),
    )
    out_specs = P("pa", "gx", "gz", None)
    return jax.shard_map(local, mesh=mesh, in_specs=in_specs, out_specs=out_specs, check_vma=False)
```

```python
import functools

import jax
import jax.numpy as jnp
from jax import lax
from jax.experimental import pallas as pl
from jax.experimental.pallas import tpu as pltpu
from jax.sharding import PartitionSpec as P


STEPS = 4
courant = 0.045
centre_coef = -7.5
near_coef = 4.0 / 3.0
far_coef = -1.0 / 12.0
middle = 1.5
ZC = 8
MESH = pl.DeviceIdType.MESH


def kernel(
    GX, GZ, PA, cells, NX, NZ,
    spread, vel_hbm, now_hbm, prev_hbm, obs_hbm, rec_hbm, out_hbm,
    natural, natural_obs, natural_rec, natural_out,
    U, V, C, W0, L, LAM, S, OB, MK,
    RV, AR, CUR, H, HR,
    in_sem, out_sem, halo_send, halo_recv, vel_send, vel_recv, ar_send, ar_recv,
    h_send, h_recv,
):
    gx, gz, pa = lax.axis_index("gx"), lax.axis_index("gz"), lax.axis_index("pa")
    core, hi = lax.rem(pa, 2), pa // 2
    partner = hi * 2 + (1 - core)
    across = (1 - hi) * 2 + core
    diagonal = (1 - hi) * 2 + (1 - core)

    loads = [
        pltpu.make_async_copy(now_hbm, natural.at[0], in_sem.at[0]),
        pltpu.make_async_copy(vel_hbm, natural.at[1], in_sem.at[1]),
        pltpu.make_async_copy(prev_hbm, natural.at[2], in_sem.at[2]),
        pltpu.make_async_copy(obs_hbm, natural_obs, in_sem.at[3]),
        pltpu.make_async_copy(rec_hbm, natural_rec, in_sem.at[4]),
    ]
    for load in loads:
        load.start()

    def turn(index, group, stride, step):
        low = lax.rem(index, stride)
        digit = lax.rem(index // stride, group)
        high = index // (stride * group)
        return (high * group + lax.rem(digit + step, group)) * stride + low

    stages = [
        [{"pa": turn(pa, 4, 1, j)} for j in (1, 2, 3)],
        [{"gz": turn(gz, GZ // 4, 4, j)} for j in range(1, GZ // 4)],
        [{"gz": turn(gz, 4, 1, j)} for j in (1, 2, 3)],
        [{"gx": turn(gx, 4, 1, j)} for j in (1, 2, 3)],
        [{"gx": turn(gx, GX // 4, 4, j)} for j in range(1, GX // 4)],
    ]
    half = [lax.rem(gz, 2), 1 - lax.rem(gz, 2)]
    z_side = [gz + 2 * h - 1 for h in half]
    has_low, has_high = gx > 0, gx < GX - 1
    has_side = [(side >= 0) & (side < GZ) for side in z_side]
    low_dest = {"gx": lax.rem(gx + GX - 1, GX)}
    high_dest = {"gx": lax.rem(gx + 1, GX)}
    side_dest = [{"gz": lax.rem(side + GZ, GZ)} for side in z_side]
    sends_halo = [has_low, has_high] + has_side
    gets_halo = [has_high, has_low] + has_side
    greet = [low_dest, high_dest] + side_dest

    barrier = pltpu.get_barrier_semaphore()
    for d in range(4):
        @pl.when(sends_halo[d])
        def _(d=d):
            pl.semaphore_signal(barrier, inc=1, device_id=greet[d], device_id_type=MESH)
    count = 0
    for stage in stages:
        for peer in stage:
            pl.semaphore_signal(barrier, inc=1, device_id=peer, device_id_type=MESH)
            count += 1

    zero_x = jnp.zeros((2, NZ, 8, 128), jnp.float32)
    zero_z = jnp.zeros((NX, 2, 8, 128), jnp.float32)

    @pl.when(gx == 0)
    def _():
        for n in range(7):
            U[n, 0:2, 2 : NZ + 2] = zero_x

    @pl.when(gx == GX - 1)
    def _():
        for n in range(7):
            U[n, NX + 2 : NX + 4, 2 : NZ + 2] = zero_x

    @pl.when(gz == 0)
    def _():
        for n in range(7):
            U[n, 2 : NX + 2, 0:2] = zero_z

    @pl.when(gz == GZ - 1)
    def _():
        for n in range(7):
            U[n, 2 : NX + 2, NZ + 2 : NZ + 4] = zero_z

    def to_tiles(read, write, first=0, planes=NX):
        def plane(x, carry):
            for zt in range(NZ // 8):
                parts = [read(k, x, zt) for k in range(8)]
                write(x, zt * 8, jnp.swapaxes(jnp.stack(parts, axis=0), 0, 1))
            return carry
        lax.fori_loop(first, first + planes, plane, 0)

    def read_wave(slot):
        def read(k, x, zt):
            y = (k % 4) * 128
            return natural[slot, k // 4, x, zt * 8 : zt * 8 + 8, y : y + 128]
        return read

    def read_plain(ref):
        def read(k, x, zt):
            y = (k % 4) * 128
            return ref[x, zt * 8 : zt * 8 + 8, y : y + 128].astype(jnp.float32)
        return read

    def write_now(x, z, tiles):
        U[0, x + 2, z + 2 : z + 10] = tiles

    def write_velocity(x, z, tiles):
        V[x, z : z + 8] = tiles
        C[x, z : z + 8] = courant * tiles * tiles

    def write_prev(x, z, tiles):
        W0[x, z : z + 8] = tiles

    def write_obs(x, z, tiles):
        OB[x, z : z + 8] = tiles

    def write_mask(x, z, tiles):
        MK[x, z : z + 8] = tiles

    def halo(n, s, d):
        field = U.at[n]
        rows = pl.ds(2 + half[s] * ZC, ZC)
        inner = pl.ds(2, NX)
        source, target, dest = [
            ((pl.ds(2, 2), rows), (pl.ds(NX + 2, 2), rows), low_dest),
            ((pl.ds(NX, 2), rows), (pl.ds(0, 2), rows), high_dest),
            (
                (inner, pl.ds(2 + half[s] * (NZ - 2), 2)),
                (inner, pl.ds((1 - half[s]) * (NZ + 2), 2)),
                side_dest[s],
            ),
        ][d]
        return pltpu.make_async_remote_copy(
            src_ref=field.at[source],
            dst_ref=field.at[target],
            send_sem=halo_send.at[n, s * 3 + d],
            recv_sem=halo_recv.at[n, s * 3 + d],
            device_id=dest,
            device_id_type=MESH,
        )

    def send_halo(n, s, d):
        @pl.when(sends_halo[d if d < 2 else 2 + s])
        def _():
            halo(n, s, d).start()

    def wait_halo(n, s, d):
        @pl.when(gets_halo[d if d < 2 else 2 + s])
        def _():
            halo(n, s, d).wait_recv()

    loads[0].wait()
    to_tiles(read_wave(0), write_now, 0, 2)
    to_tiles(read_wave(0), write_now, NX - 2, 2)
    peers = count
    for gets in gets_halo:
        peers = peers + jnp.where(gets, 1, 0)
    pl.semaphore_wait(barrier, peers)
    for s in (0, 1):
        for d in (0, 1):
            send_halo(0, s, d)
    to_tiles(read_wave(0), write_now, 2, NX - 4)
    for s in (0, 1):
        send_halo(0, s, 2)

    loads[1].wait()
    to_tiles(read_wave(1), write_velocity)

    slab = NX // PA
    vel_copies = []
    for j in (1, 2, 3):
        q = lax.rem(pa + j, PA)
        vel_copies.append(
            pltpu.make_async_remote_copy(
                src_ref=V.at[pl.ds(q * slab, slab)],
                dst_ref=RV.at[j],
                send_sem=vel_send.at[j],
                recv_sem=vel_recv.at[j],
                device_id={"pa": q},
                device_id_type=MESH,
            )
        )
    for copy in vel_copies:
        copy.start()

    loads[2].wait()
    to_tiles(read_wave(2), write_prev)
    loads[3].wait()
    to_tiles(read_plain(natural_obs), write_obs)
    loads[4].wait()
    to_tiles(read_plain(natural_rec), write_mask)

    shape = (ZC, 8, 128)
    lane = lax.broadcasted_iota(jnp.int32, shape, 2)
    sub = lax.broadcasted_iota(jnp.int32, shape, 1)
    lane2 = lax.broadcasted_iota(jnp.int32, (8, 128), 1)
    sub2 = lax.broadcasted_iota(jnp.int32, (8, 128), 0)

    scale = (
        jnp.full((8, 128), spread[0], jnp.int32).astype(jnp.float32)
        / jnp.full((8, 128), spread[1], jnp.int32).astype(jnp.float32)
    )
    pull = 2.0 / scale

    def laplace(n, x, z):
        here = U[n, x + 2, pl.ds(z + 2, ZC)]
        near = U[n, x + 1, pl.ds(z + 2, ZC)] + U[n, x + 3, pl.ds(z + 2, ZC)]
        far = U[n, x, pl.ds(z + 2, ZC)] + U[n, x + 4, pl.ds(z + 2, ZC)]
        near = near + (U[n, x + 2, pl.ds(z + 1, ZC)] + U[n, x + 2, pl.ds(z + 3, ZC)])
        far = far + (U[n, x + 2, pl.ds(z, ZC)] + U[n, x + 2, pl.ds(z + 4, ZC)])
        before = pltpu.roll(here, 1, 1)
        before = jnp.where((sub == 0) | (sub == 4), 0.0, before)
        after = pltpu.roll(here, 7, 1)
        after = jnp.where((sub == 3) | (sub == 7), 0.0, after)
        near = near + (
            pltpu.roll(jnp.where(lane == 127, before, here), 1, 2)
            + pltpu.roll(jnp.where(lane == 0, after, here), 127, 2)
        )
        far = far + (
            pltpu.roll(jnp.where(lane >= 126, before, here), 2, 2)
            + pltpu.roll(jnp.where(lane <= 1, after, here), 126, 2)
        )
        return here, centre_coef * here + near_coef * near + far_coef * far

    def advance(n, x, z):
        here, applied = laplace(n, x, z)
        at = (x, pl.ds(z, ZC))
        inner = (x + 2, pl.ds(z + 2, ZC))
        if n < STEPS:
            older = W0[at] if n == 0 else U[(n - 1,) + inner]
            newer = 2.0 * here - older + C[at] * applied
            if n < STEPS - 1:
                L[(n,) + at] = applied
                U[(n + 1,) + inner] = newer
            else:
                adjoint = MK[at] * (newer - OB[at])
                S[at] = adjoint * applied
                LAM[(0,) + at] = adjoint
                U[(n + 1,) + inner] = C[at] * adjoint
        else:
            k = n - STEPS
            adjoint = 2.0 * LAM[(k,) + at] + applied
            if k > 0:
                adjoint = adjoint - LAM[(k - 1,) + at]
            total = S[at] + adjoint * L[(STEPS - 2 - k,) + at]
            if k < STEPS - 2:
                S[at] = total
                LAM[(k + 1,) + at] = adjoint
                U[(n + 1,) + inner] = C[at] * adjoint
            else:
                velocity = V[at]
                H[at] = (2.0 * courant) * velocity * total + pull[None] * (velocity - middle)

    def planes(n, s, first, count_x):
        def body(x, carry):
            advance(n, x, half[s] * ZC)
            return carry
        lax.fori_loop(first, first + count_x, body, 0)

    def ar_copies(stage):
        return [
            pltpu.make_async_remote_copy(
                src_ref=CUR.at[stage],
                dst_ref=AR.at[stage, j],
                send_sem=ar_send.at[stage, j],
                recv_sem=ar_recv.at[stage, j],
                device_id=peer,
                device_id_type=MESH,
            )
            for j, peer in enumerate(stages[stage])
        ]

    def ar_start(stage):
        for copy in ar_copies(stage):
            copy.start()

    def ar_finish(stage):
        total = CUR[stage]
        for j, copy in enumerate(ar_copies(stage)):
            copy.wait_recv()
            total = total + AR[stage, j]
        CUR[stage + 1] = total

    def pair_sums():
        for copy in vel_copies:
            copy.wait_recv()

        def body(i, sums):
            x, z = i // NZ, lax.rem(i, NZ)
            tile = [V[pa * slab + x, z]] + [RV[j, x, z] for j in (1, 2, 3)]
            swapped = [pltpu.roll(t, 4, 0) for t in tile]
            out, at = [], 0
            for a in range(4):
                for b in range(a, 4):
                    if b > a:
                        delta = tile[a] - tile[b]
                        out.append(sums[at] + delta * delta)
                        at += 1
                    delta = tile[a] - swapped[b]
                    out.append(sums[at] + delta * delta)
                    at += 1
            return tuple(out)

        zero = jnp.zeros((8, 128), jnp.float32)
        sums = lax.fori_loop(0, slab * NZ, body, (zero,) * 16)
        groups = [lax.rem(pa + PA - j, PA) for j in range(4)]
        table, at = zero, 0
        for a in range(4):
            for b in range(a, 4):
                if b > a:
                    plain = jnp.sum(sums[at], axis=1, keepdims=True)
                    at += 1
                    spot = (lane2 == groups[a] * 8 + groups[b] * 2) | (lane2 == groups[b] * 8 + groups[a] * 2)
                    table = jnp.where(spot, plain, table)
                crossed = jnp.sum(sums[at], axis=1, keepdims=True)
                at += 1
                table = jnp.where(lane2 == groups[a] * 8 + groups[b] * 2 + 1, crossed, table)
                if b > a:
                    turned = pltpu.roll(jnp.broadcast_to(crossed, (8, 128)), 4, 0)
                    table = jnp.where(lane2 == groups[b] * 8 + groups[a] * 2 + 1, turned, table)
        CUR[0] = table

    firsts = [2, 4, 0, NX - 2]

    def chunk(c):
        return pl.ds(firsts[c % 4], 2), pl.ds(half[c // 4] * ZC, ZC)

    def h_copy(kind, c, src, dest):
        return pltpu.make_async_remote_copy(
            src_ref=src,
            dst_ref=HR.at[kind, c],
            send_sem=h_send.at[kind, c],
            recv_sem=h_recv.at[kind, c],
            device_id={"pa": dest},
            device_id_type=MESH,
        )

    def h_own(c):
        return h_copy(0, c, H.at[chunk(c)], partner)

    def h_across(c):
        return h_copy(1, c, H.at[chunk(c)], across)

    def h_forward(c):
        return h_copy(2, c, HR.at[1, c], partner)

    def h_start(c):
        h_across(c).start()
        h_own(c).start()

    for n in range(7):
        for s in (0, 1):
            wait_halo(n, s, 2)
            planes(n, s, 2, NX - 4)
            if n == 6:
                h_start(4 * s)
                h_start(4 * s + 1)
            wait_halo(n, s, 0)
            wait_halo(n, s, 1)
            planes(n, s, 0, 2)
            if n < 6:
                send_halo(n + 1, s, 0)
            else:
                h_start(4 * s + 2)
            planes(n, s, NX - 2, 2)
            if n < 6:
                send_halo(n + 1, s, 1)
                send_halo(n + 1, s, 2)
            else:
                h_start(4 * s + 3)
        if n == 2:
            pair_sums()
            ar_start(0)
        elif n > 2:
            ar_finish(n - 3)
            ar_start(n - 2)

    chunks = range(8)
    for c in chunks:
        h_across(c).wait_recv()
        h_forward(c).start()
    ar_finish(4)

    table = CUR[5]
    low = jnp.sum(jnp.where(sub2 < 4, table, 0.0), axis=0, keepdims=True)
    high = jnp.sum(jnp.where(sub2 < 4, 0.0, table), axis=0, keepdims=True)
    weight = jnp.exp(-(jnp.where(sub2 < 4, low, high) / cells) / scale)

    def column(index):
        picked = jnp.sum(jnp.where(lane2 == index, weight, 0.0), axis=1, keepdims=True)
        return jnp.broadcast_to(picked, (8, 128))

    groups = [pa, partner, across, diagonal]
    plain = [column(pa * 8 + g * 2) for g in groups]
    crossed = [column(pa * 8 + g * 2 + 1) for g in groups]
    all_weights = plain[0] + crossed[0]
    for g in (1, 2, 3):
        all_weights = all_weights + (plain[g] + crossed[g])
    count_all = 2 * PA
    own = pull * all_weights / count_all
    plain = [-w / count_all for w in plain]
    crossed = [-w / count_all for w in crossed]

    outs = []
    for c in chunks:
        h_own(c).wait_recv()
        h_forward(c).wait_recv()
        x0, z = firsts[c % 4], pl.multiple_of(half[c // 4] * ZC, ZC)
        for i in range(2):
            x = x0 + i
            result = own[None] * (V[x, pl.ds(z, ZC)] - middle)
            for g in range(4):
                tile = H[x, pl.ds(z, ZC)] if g == 0 else HR[g - 1, c, i]
                result = result + plain[g][None] * tile + crossed[g][None] * pltpu.roll(tile, 4, 1)
            result = jnp.swapaxes(result, 0, 1)
            for k in range(8):
                y = (k % 4) * 128
                natural_out[k // 4, x, pl.ds(z, ZC), y : y + 128] = result[k]
        at = (slice(None), pl.ds(x0, 2), pl.ds(z, ZC))
        copy = pltpu.make_async_copy(natural_out.at[at], out_hbm.at[at], out_sem.at[c])
        copy.start()
        outs.append(copy)

    for n in range(7):
        for s in (0, 1):
            for d in range(3):
                @pl.when(sends_halo[d if d < 2 else 2 + s])
                def _(n=n, s=s, d=d):
                    halo(n, s, d).wait_send()
    for copy in vel_copies:
        copy.wait_send()
    for stage in range(5):
        for copy in ar_copies(stage):
            copy.wait_send()
    for c in chunks:
        h_across(c).wait_send()
        h_own(c).wait_send()
        h_forward(c).wait_send()
    for copy in outs:
        copy.wait()


def local(velocity, wave_now, wave_prev, observed, receiver, spread):
    GX, GZ, PA = lax.axis_size("gx"), lax.axis_size("gz"), lax.axis_size("pa")
    particles, NX, NZ, NY = velocity.shape
    cells = float(NX * GX * NZ * GZ * NY)
    any_space = pl.BlockSpec(memory_space=pl.ANY)
    tiles = (NX, NZ, 8, 128)
    f32 = jnp.float32
    dma = pltpu.SemaphoreType.DMA
    return pl.pallas_call(
        functools.partial(kernel, GX, GZ, PA, cells, NX, NZ),
        out_shape=jax.ShapeDtypeStruct(velocity.shape, f32),
        in_specs=[pl.BlockSpec(memory_space=pltpu.SMEM)] + [any_space] * 5,
        out_specs=any_space,
        scratch_shapes=[
            pltpu.VMEM((3,) + velocity.shape, f32),
            pltpu.VMEM(observed.shape, f32),
            pltpu.VMEM(receiver.shape, jnp.int32),
            pltpu.VMEM(velocity.shape, f32),
            pltpu.VMEM((7, NX + 4, NZ + 4, 8, 128), f32),
            pltpu.VMEM(tiles, f32),
            pltpu.VMEM(tiles, f32),
            pltpu.VMEM(tiles, f32),
            pltpu.VMEM((3,) + tiles, f32),
            pltpu.VMEM((3,) + tiles, f32),
            pltpu.VMEM(tiles, f32),
            pltpu.VMEM(tiles, f32),
            pltpu.VMEM(tiles, f32),
            pltpu.VMEM((4, NX // PA, NZ, 8, 128), f32),
            pltpu.VMEM((5, 3, 8, 128), f32),
            pltpu.VMEM((6, 8, 128), f32),
            pltpu.VMEM(tiles, f32),
            pltpu.VMEM((3, 8, 2, ZC, 8, 128), f32),
            dma((5,)),
            dma((8,)),
            dma((7, 6)),
            dma((7, 6)),
            dma((4,)),
            dma((4,)),
            dma((5, 3)),
            dma((5, 3)),
            dma((3, 8)),
            dma((3, 8)),
        ],
        compiler_params=pltpu.CompilerParams(collective_id=0, has_side_effects=True),
    )(spread, velocity, wave_now, wave_prev, observed, receiver)


def solution(mesh):
    in_specs = (
        P("pa", "gx", "gz", None),
        P("pa", "gx", "gz", None),
        P("pa", "gx", "gz", None),
        P("gx", "gz", None),
        P("gx", "gz", None),
        P(),
    )
    out_specs = P("pa", "gx", "gz", None)
    return jax.shard_map(local, mesh=mesh, in_specs=in_specs, out_specs=out_specs, check_vma=False)
```

```python
import functools

import jax
import jax.numpy as jnp
from jax import lax
from jax.experimental import pallas as pl
from jax.experimental.pallas import tpu as pltpu
from jax.sharding import PartitionSpec as P


STEPS = 4
courant = 0.045
centre_coef = -7.5
near_coef = 4.0 / 3.0
far_coef = -1.0 / 12.0
middle = 1.5
ZC = 8
MESH = pl.DeviceIdType.MESH


def kernel(
    GX, GZ, PA, cells, NX, NZ,
    spread, vel_hbm, now_hbm, prev_hbm, obs_hbm, rec_hbm, out_hbm,
    natural, natural_obs, natural_rec, natural_out,
    U, V, C, W0, L, LAM, S, OB, MK,
    RV, AR, CUR, H, HR, RL,
    in_sem, out_sem, halo_send, halo_recv, vel_send, vel_recv, ar_send, ar_recv,
    h_send, h_recv, relay_send, relay_recv,
):
    gx, gz, pa = lax.axis_index("gx"), lax.axis_index("gz"), lax.axis_index("pa")
    core, hi = lax.rem(pa, 2), pa // 2
    partner = hi * 2 + (1 - core)
    across = (1 - hi) * 2 + core
    diagonal = (1 - hi) * 2 + (1 - core)

    loads = [
        pltpu.make_async_copy(now_hbm, natural.at[0], in_sem.at[0]),
        pltpu.make_async_copy(vel_hbm, natural.at[1], in_sem.at[1]),
        pltpu.make_async_copy(prev_hbm, natural.at[2], in_sem.at[2]),
        pltpu.make_async_copy(obs_hbm, natural_obs, in_sem.at[3]),
        pltpu.make_async_copy(rec_hbm, natural_rec, in_sem.at[4]),
    ]
    for load in loads:
        load.start()

    def turn(index, group, stride, step):
        low = lax.rem(index, stride)
        digit = lax.rem(index // stride, group)
        high = index // (stride * group)
        return (high * group + lax.rem(digit + step, group)) * stride + low

    stages = [
        [{"pa": turn(pa, 4, 1, j)} for j in (1, 2, 3)],
        [{"gz": turn(gz, GZ // 4, 4, j)} for j in range(1, GZ // 4)],
        [{"gz": turn(gz, 4, 1, j)} for j in (1, 2, 3)],
        [{"gx": turn(gx, 4, 1, j)} for j in (1, 2, 3)],
        [{"gx": turn(gx, GX // 4, 4, j)} for j in range(1, GX // 4)],
    ]
    half = [lax.rem(gz, 2), 1 - lax.rem(gz, 2)]
    z_side = [gz + 2 * h - 1 for h in half]
    has_low, has_high = gx > 0, gx < GX - 1
    has_side = [(side >= 0) & (side < GZ) for side in z_side]
    low_dest = {"gx": lax.rem(gx + GX - 1, GX)}
    high_dest = {"gx": lax.rem(gx + 1, GX)}
    side_dest = [{"gz": lax.rem(side + GZ, GZ)} for side in z_side]
    sends_halo = [has_low, has_high] + has_side
    gets_halo = [has_high, has_low] + has_side
    greet = [low_dest, high_dest] + side_dest

    barrier = pltpu.get_barrier_semaphore()
    for d in range(4):
        @pl.when(sends_halo[d])
        def _(d=d):
            pl.semaphore_signal(barrier, inc=1, device_id=greet[d], device_id_type=MESH)
    count = 0
    for stage in stages:
        for peer in stage:
            pl.semaphore_signal(barrier, inc=1, device_id=peer, device_id_type=MESH)
            count += 1
    beside = lax.rem(gz + 4, GZ)
    pl.semaphore_signal(
        barrier, inc=1, device_id={"gz": beside, "pa": across}, device_id_type=MESH
    )
    count += 1

    zero_x = jnp.zeros((2, NZ, 8, 128), jnp.float32)
    zero_z = jnp.zeros((NX, 2, 8, 128), jnp.float32)

    @pl.when(gx == 0)
    def _():
        for n in range(7):
            U[n, 0:2, 2 : NZ + 2] = zero_x

    @pl.when(gx == GX - 1)
    def _():
        for n in range(7):
            U[n, NX + 2 : NX + 4, 2 : NZ + 2] = zero_x

    @pl.when(gz == 0)
    def _():
        for n in range(7):
            U[n, 2 : NX + 2, 0:2] = zero_z

    @pl.when(gz == GZ - 1)
    def _():
        for n in range(7):
            U[n, 2 : NX + 2, NZ + 2 : NZ + 4] = zero_z

    def to_tiles(read, write, first=0, planes=NX):
        def plane(x, carry):
            for zt in range(NZ // 8):
                parts = [read(k, x, zt) for k in range(8)]
                write(x, zt * 8, jnp.swapaxes(jnp.stack(parts, axis=0), 0, 1))
            return carry
        lax.fori_loop(first, first + planes, plane, 0)

    def read_wave(slot):
        def read(k, x, zt):
            y = (k % 4) * 128
            return natural[slot, k // 4, x, zt * 8 : zt * 8 + 8, y : y + 128]
        return read

    def read_plain(ref):
        def read(k, x, zt):
            y = (k % 4) * 128
            return ref[x, zt * 8 : zt * 8 + 8, y : y + 128].astype(jnp.float32)
        return read

    def write_now(x, z, tiles):
        U[0, x + 2, z + 2 : z + 10] = tiles

    def write_velocity(x, z, tiles):
        V[x, z : z + 8] = tiles
        C[x, z : z + 8] = courant * tiles * tiles

    def write_prev(x, z, tiles):
        W0[x, z : z + 8] = tiles

    def write_obs(x, z, tiles):
        OB[x, z : z + 8] = tiles

    def write_mask(x, z, tiles):
        MK[x, z : z + 8] = tiles

    def halo(n, s, d):
        field = U.at[n]
        rows = pl.ds(2 + half[s] * ZC, ZC)
        inner = pl.ds(2, NX)
        source, target, dest = [
            ((pl.ds(2, 2), rows), (pl.ds(NX + 2, 2), rows), low_dest),
            ((pl.ds(NX, 2), rows), (pl.ds(0, 2), rows), high_dest),
            (
                (inner, pl.ds(2 + half[s] * (NZ - 2), 2)),
                (inner, pl.ds((1 - half[s]) * (NZ + 2), 2)),
                side_dest[s],
            ),
        ][d]
        return pltpu.make_async_remote_copy(
            src_ref=field.at[source],
            dst_ref=field.at[target],
            send_sem=halo_send.at[n, s * 3 + d],
            recv_sem=halo_recv.at[n, s * 3 + d],
            device_id=dest,
            device_id_type=MESH,
        )

    def send_halo(n, s, d):
        @pl.when(sends_halo[d if d < 2 else 2 + s])
        def _():
            halo(n, s, d).start()

    def wait_halo(n, s, d):
        @pl.when(gets_halo[d if d < 2 else 2 + s])
        def _():
            halo(n, s, d).wait_recv()

    loads[0].wait()
    to_tiles(read_wave(0), write_now, 0, 2)
    to_tiles(read_wave(0), write_now, NX - 2, 2)
    peers = count
    for gets in gets_halo:
        peers = peers + jnp.where(gets, 1, 0)
    pl.semaphore_wait(barrier, peers)
    for s in (0, 1):
        for d in (0, 1):
            send_halo(0, s, d)
    to_tiles(read_wave(0), write_now, 2, NX - 4)
    for s in (0, 1):
        send_halo(0, s, 2)

    loads[1].wait()
    to_tiles(read_wave(1), write_velocity)

    slab = NX // PA
    vel_copies = []
    for j in (1, 2, 3):
        q = lax.rem(pa + j, PA)
        vel_copies.append(
            pltpu.make_async_remote_copy(
                src_ref=V.at[pl.ds(q * slab, slab)],
                dst_ref=RV.at[j],
                send_sem=vel_send.at[j],
                recv_sem=vel_recv.at[j],
                device_id={"pa": q},
                device_id_type=MESH,
            )
        )
    for copy in vel_copies:
        copy.start()

    loads[2].wait()
    to_tiles(read_wave(2), write_prev)
    loads[3].wait()
    to_tiles(read_plain(natural_obs), write_obs)
    loads[4].wait()
    to_tiles(read_plain(natural_rec), write_mask)

    shape = (ZC, 8, 128)
    lane = lax.broadcasted_iota(jnp.int32, shape, 2)
    sub = lax.broadcasted_iota(jnp.int32, shape, 1)
    lane2 = lax.broadcasted_iota(jnp.int32, (8, 128), 1)
    sub2 = lax.broadcasted_iota(jnp.int32, (8, 128), 0)

    scale = (
        jnp.full((8, 128), spread[0], jnp.int32).astype(jnp.float32)
        / jnp.full((8, 128), spread[1], jnp.int32).astype(jnp.float32)
    )
    pull = 2.0 / scale

    def laplace(n, x, z):
        here = U[n, x + 2, pl.ds(z + 2, ZC)]
        near = U[n, x + 1, pl.ds(z + 2, ZC)] + U[n, x + 3, pl.ds(z + 2, ZC)]
        far = U[n, x, pl.ds(z + 2, ZC)] + U[n, x + 4, pl.ds(z + 2, ZC)]
        near = near + (U[n, x + 2, pl.ds(z + 1, ZC)] + U[n, x + 2, pl.ds(z + 3, ZC)])
        far = far + (U[n, x + 2, pl.ds(z, ZC)] + U[n, x + 2, pl.ds(z + 4, ZC)])
        before = pltpu.roll(here, 1, 1)
        before = jnp.where((sub == 0) | (sub == 4), 0.0, before)
        after = pltpu.roll(here, 7, 1)
        after = jnp.where((sub == 3) | (sub == 7), 0.0, after)
        near = near + (
            pltpu.roll(jnp.where(lane == 127, before, here), 1, 2)
            + pltpu.roll(jnp.where(lane == 0, after, here), 127, 2)
        )
        far = far + (
            pltpu.roll(jnp.where(lane >= 126, before, here), 2, 2)
            + pltpu.roll(jnp.where(lane <= 1, after, here), 126, 2)
        )
        return here, centre_coef * here + near_coef * near + far_coef * far

    def advance(n, x, z):
        here, applied = laplace(n, x, z)
        at = (x, pl.ds(z, ZC))
        inner = (x + 2, pl.ds(z + 2, ZC))
        if n < STEPS:
            older = W0[at] if n == 0 else U[(n - 1,) + inner]
            newer = 2.0 * here - older + C[at] * applied
            if n < STEPS - 1:
                L[(n,) + at] = applied
                U[(n + 1,) + inner] = newer
            else:
                adjoint = MK[at] * (newer - OB[at])
                S[at] = adjoint * applied
                LAM[(0,) + at] = adjoint
                U[(n + 1,) + inner] = C[at] * adjoint
        else:
            k = n - STEPS
            adjoint = 2.0 * LAM[(k,) + at] + applied
            if k > 0:
                adjoint = adjoint - LAM[(k - 1,) + at]
            total = S[at] + adjoint * L[(STEPS - 2 - k,) + at]
            if k < STEPS - 2:
                S[at] = total
                LAM[(k + 1,) + at] = adjoint
                U[(n + 1,) + inner] = C[at] * adjoint
            else:
                velocity = V[at]
                H[at] = (2.0 * courant) * velocity * total + pull[None] * (velocity - middle)

    def planes(n, s, first, count_x):
        def body(x, carry):
            advance(n, x, half[s] * ZC)
            return carry
        lax.fori_loop(first, first + count_x, body, 0)

    def ar_copies(stage):
        return [
            pltpu.make_async_remote_copy(
                src_ref=CUR.at[stage],
                dst_ref=AR.at[stage, j],
                send_sem=ar_send.at[stage, j],
                recv_sem=ar_recv.at[stage, j],
                device_id=peer,
                device_id_type=MESH,
            )
            for j, peer in enumerate(stages[stage])
        ]

    def ar_start(stage):
        for copy in ar_copies(stage):
            copy.start()

    def ar_finish(stage):
        total = CUR[stage]
        for j, copy in enumerate(ar_copies(stage)):
            copy.wait_recv()
            total = total + AR[stage, j]
        CUR[stage + 1] = total

    def pair_sums():
        for copy in vel_copies:
            copy.wait_recv()

        def body(i, sums):
            x, z = i // NZ, lax.rem(i, NZ)
            tile = [V[pa * slab + x, z]] + [RV[j, x, z] for j in (1, 2, 3)]
            swapped = [pltpu.roll(t, 4, 0) for t in tile]
            out, at = [], 0
            for a in range(4):
                for b in range(a, 4):
                    if b > a:
                        delta = tile[a] - tile[b]
                        out.append(sums[at] + delta * delta)
                        at += 1
                    delta = tile[a] - swapped[b]
                    out.append(sums[at] + delta * delta)
                    at += 1
            return tuple(out)

        zero = jnp.zeros((8, 128), jnp.float32)
        sums = lax.fori_loop(0, slab * NZ, body, (zero,) * 16)
        groups = [lax.rem(pa + PA - j, PA) for j in range(4)]
        table, at = zero, 0
        for a in range(4):
            for b in range(a, 4):
                if b > a:
                    plain = jnp.sum(sums[at], axis=1, keepdims=True)
                    at += 1
                    spot = (lane2 == groups[a] * 8 + groups[b] * 2) | (lane2 == groups[b] * 8 + groups[a] * 2)
                    table = jnp.where(spot, plain, table)
                crossed = jnp.sum(sums[at], axis=1, keepdims=True)
                at += 1
                table = jnp.where(lane2 == groups[a] * 8 + groups[b] * 2 + 1, crossed, table)
                if b > a:
                    turned = pltpu.roll(jnp.broadcast_to(crossed, (8, 128)), 4, 0)
                    table = jnp.where(lane2 == groups[b] * 8 + groups[a] * 2 + 1, turned, table)
        CUR[0] = table

    firsts = [2, 4, 0, NX - 2]

    def chunk(c):
        return pl.ds(firsts[c % 4], 2), pl.ds(half[c // 4] * ZC, ZC)

    def h_copy(kind, c, src, dest):
        return pltpu.make_async_remote_copy(
            src_ref=src,
            dst_ref=HR.at[kind, c],
            send_sem=h_send.at[kind, c],
            recv_sem=h_recv.at[kind, c],
            device_id={"pa": dest},
            device_id_type=MESH,
        )

    def h_own(c):
        return h_copy(0, c, H.at[chunk(c)], partner)

    def h_relay(c):
        return pltpu.make_async_remote_copy(
            src_ref=H.at[chunk(c)],
            dst_ref=RL.at[hi, c // 2],
            send_sem=relay_send.at[c],
            recv_sem=relay_recv.at[hi, c // 2],
            device_id={"gz": beside, "pa": (c % 2) * 2 + core},
            device_id_type=MESH,
        )

    def relayed(source, i):
        return pltpu.make_async_remote_copy(
            src_ref=H.at[chunk(2 * i)],
            dst_ref=RL.at[source, i],
            send_sem=relay_send.at[2 * i],
            recv_sem=relay_recv.at[source, i],
            device_id={"gz": beside, "pa": source * 2 + core},
            device_id_type=MESH,
        )

    def h_pass(source, i):
        c = 2 * i + hi
        return pltpu.make_async_remote_copy(
            src_ref=RL.at[source, i],
            dst_ref=HR.at[1, c],
            send_sem=relay_send.at[8 + source * 4 + i],
            recv_sem=h_recv.at[1, c],
            device_id={"gz": beside, "pa": (1 - source) * 2 + core},
            device_id_type=MESH,
        )

    def h_across(c):
        return h_copy(1, c, H.at[chunk(c)], across)

    def h_forward(c):
        return h_copy(2, c, HR.at[1, c], partner)

    def h_start(c):
        h_relay(c).start()
        h_own(c).start()

    for n in range(7):
        for s in (0, 1):
            wait_halo(n, s, 2)
            planes(n, s, 2, NX - 4)
            if n == 6:
                h_start(4 * s)
                h_start(4 * s + 1)
            wait_halo(n, s, 0)
            wait_halo(n, s, 1)
            planes(n, s, 0, 2)
            if n < 6:
                send_halo(n + 1, s, 0)
            else:
                h_start(4 * s + 2)
            planes(n, s, NX - 2, 2)
            if n < 6:
                send_halo(n + 1, s, 1)
                send_halo(n + 1, s, 2)
            else:
                h_start(4 * s + 3)
        if n == 2:
            pair_sums()
            ar_start(0)
        elif n > 2:
            ar_finish(n - 3)
            ar_start(n - 2)

    chunks = range(8)
    def pass_on(i):
        for source in (0, 1):
            relayed(source, i).wait_recv()
            h_pass(source, i).start()

    def forward(i):
        for c in (2 * i, 2 * i + 1):
            h_across(c).wait_recv()
            h_forward(c).start()

    pass_on(0)
    pass_on(1)
    forward(0)
    pass_on(2)
    forward(1)
    pass_on(3)
    forward(2)
    forward(3)
    ar_finish(4)

    table = CUR[5]
    low = jnp.sum(jnp.where(sub2 < 4, table, 0.0), axis=0, keepdims=True)
    high = jnp.sum(jnp.where(sub2 < 4, 0.0, table), axis=0, keepdims=True)
    weight = jnp.exp(-(jnp.where(sub2 < 4, low, high) / cells) / scale)

    def column(index):
        picked = jnp.sum(jnp.where(lane2 == index, weight, 0.0), axis=1, keepdims=True)
        return jnp.broadcast_to(picked, (8, 128))

    groups = [pa, partner, across, diagonal]
    plain = [column(pa * 8 + g * 2) for g in groups]
    crossed = [column(pa * 8 + g * 2 + 1) for g in groups]
    all_weights = plain[0] + crossed[0]
    for g in (1, 2, 3):
        all_weights = all_weights + (plain[g] + crossed[g])
    count_all = 2 * PA
    own = pull * all_weights / count_all
    plain = [-w / count_all for w in plain]
    crossed = [-w / count_all for w in crossed]

    outs = []
    for c in chunks:
        h_own(c).wait_recv()
        h_forward(c).wait_recv()
        x0, z = firsts[c % 4], pl.multiple_of(half[c // 4] * ZC, ZC)
        for i in range(2):
            x = x0 + i
            result = own[None] * (V[x, pl.ds(z, ZC)] - middle)
            for g in range(4):
                tile = H[x, pl.ds(z, ZC)] if g == 0 else HR[g - 1, c, i]
                result = result + plain[g][None] * tile + crossed[g][None] * pltpu.roll(tile, 4, 1)
            result = jnp.swapaxes(result, 0, 1)
            for k in range(8):
                y = (k % 4) * 128
                natural_out[k // 4, x, pl.ds(z, ZC), y : y + 128] = result[k]
        at = (slice(None), pl.ds(x0, 2), pl.ds(z, ZC))
        copy = pltpu.make_async_copy(natural_out.at[at], out_hbm.at[at], out_sem.at[c])
        copy.start()
        outs.append(copy)

    for n in range(7):
        for s in (0, 1):
            for d in range(3):
                @pl.when(sends_halo[d if d < 2 else 2 + s])
                def _(n=n, s=s, d=d):
                    halo(n, s, d).wait_send()
    for copy in vel_copies:
        copy.wait_send()
    for stage in range(5):
        for copy in ar_copies(stage):
            copy.wait_send()
    for c in chunks:
        h_relay(c).wait_send()
        h_pass(c // 4, c % 4).wait_send()
        h_own(c).wait_send()
        h_forward(c).wait_send()
    for copy in outs:
        copy.wait()


def local(velocity, wave_now, wave_prev, observed, receiver, spread):
    GX, GZ, PA = lax.axis_size("gx"), lax.axis_size("gz"), lax.axis_size("pa")
    particles, NX, NZ, NY = velocity.shape
    cells = float(NX * GX * NZ * GZ * NY)
    any_space = pl.BlockSpec(memory_space=pl.ANY)
    tiles = (NX, NZ, 8, 128)
    f32 = jnp.float32
    dma = pltpu.SemaphoreType.DMA
    return pl.pallas_call(
        functools.partial(kernel, GX, GZ, PA, cells, NX, NZ),
        out_shape=jax.ShapeDtypeStruct(velocity.shape, f32),
        in_specs=[pl.BlockSpec(memory_space=pltpu.SMEM)] + [any_space] * 5,
        out_specs=any_space,
        scratch_shapes=[
            pltpu.VMEM((3,) + velocity.shape, f32),
            pltpu.VMEM(observed.shape, f32),
            pltpu.VMEM(receiver.shape, jnp.int32),
            pltpu.VMEM(velocity.shape, f32),
            pltpu.VMEM((7, NX + 4, NZ + 4, 8, 128), f32),
            pltpu.VMEM(tiles, f32),
            pltpu.VMEM(tiles, f32),
            pltpu.VMEM(tiles, f32),
            pltpu.VMEM((3,) + tiles, f32),
            pltpu.VMEM((3,) + tiles, f32),
            pltpu.VMEM(tiles, f32),
            pltpu.VMEM(tiles, f32),
            pltpu.VMEM(tiles, f32),
            pltpu.VMEM((4, NX // PA, NZ, 8, 128), f32),
            pltpu.VMEM((5, 3, 8, 128), f32),
            pltpu.VMEM((6, 8, 128), f32),
            pltpu.VMEM(tiles, f32),
            pltpu.VMEM((3, 8, 2, ZC, 8, 128), f32),
            pltpu.VMEM((2, 4, 2, ZC, 8, 128), f32),
            dma((5,)),
            dma((8,)),
            dma((7, 6)),
            dma((7, 6)),
            dma((4,)),
            dma((4,)),
            dma((5, 3)),
            dma((5, 3)),
            dma((3, 8)),
            dma((3, 8)),
            dma((16,)),
            dma((2, 4)),
        ],
        compiler_params=pltpu.CompilerParams(collective_id=0, has_side_effects=True),
    )(spread, velocity, wave_now, wave_prev, observed, receiver)


def solution(mesh):
    in_specs = (
        P("pa", "gx", "gz", None),
        P("pa", "gx", "gz", None),
        P("pa", "gx", "gz", None),
        P("gx", "gz", None),
        P("gx", "gz", None),
        P(),
    )
    out_specs = P("pa", "gx", "gz", None)
    return jax.shard_map(local, mesh=mesh, in_specs=in_specs, out_specs=out_specs, check_vma=False)
```

```python
import functools

import jax
import jax.numpy as jnp
from jax import lax
from jax.experimental import pallas as pl
from jax.experimental.pallas import tpu as pltpu
from jax.sharding import PartitionSpec as P


STEPS = 4
courant = 0.045
centre_coef = -7.5
near_coef = 4.0 / 3.0
far_coef = -1.0 / 12.0
middle = 1.5
ZC = 8
MESH = pl.DeviceIdType.MESH


def kernel(
    GX, GZ, PA, cells, NX, NZ,
    spread, vel_hbm, now_hbm, prev_hbm, obs_hbm, rec_hbm, out_hbm,
    natural, natural_obs, natural_rec, natural_out,
    U, V, C, W0, L, LAM, S, OB, MK,
    RV, AR, CUR, H, HR,
    in_sem, out_sem, halo_send, halo_recv, vel_send, vel_recv, ar_send, ar_recv,
    h_send, h_recv,
):
    gx, gz, pa = lax.axis_index("gx"), lax.axis_index("gz"), lax.axis_index("pa")
    core, hi = lax.rem(pa, 2), pa // 2
    partner = hi * 2 + (1 - core)
    across = (1 - hi) * 2 + core
    diagonal = (1 - hi) * 2 + (1 - core)

    loads = [
        pltpu.make_async_copy(now_hbm, natural.at[0], in_sem.at[0]),
        pltpu.make_async_copy(vel_hbm, natural.at[1], in_sem.at[1]),
        pltpu.make_async_copy(prev_hbm, natural.at[2], in_sem.at[2]),
        pltpu.make_async_copy(obs_hbm, natural_obs, in_sem.at[3]),
        pltpu.make_async_copy(rec_hbm, natural_rec, in_sem.at[4]),
    ]
    for load in loads:
        load.start()

    def turn(index, group, stride, step):
        low = lax.rem(index, stride)
        digit = lax.rem(index // stride, group)
        high = index // (stride * group)
        return (high * group + lax.rem(digit + step, group)) * stride + low

    def flip(index, stride):
        return index + stride * (1 - 2 * lax.rem(index // stride, 2))

    stages = [
        [{"pa": turn(pa, PA, 1, j)} for j in range(1, PA)],
        [{"gz": turn(gz, GZ, 1, j)} for j in range(1, GZ)],
        [{"gx": turn(gx, 4, 1, j)} for j in (1, 2, 3)],
        [{"gx": flip(gx, 4)}],
        [{"gx": flip(gx, 8)}],
    ]
    half = [lax.rem(gz, 2), 1 - lax.rem(gz, 2)]
    z_side = [gz + 2 * h - 1 for h in half]
    has_low, has_high = gx > 0, gx < GX - 1
    has_side = [(side >= 0) & (side < GZ) for side in z_side]
    low_dest = {"gx": lax.rem(gx + GX - 1, GX)}
    high_dest = {"gx": lax.rem(gx + 1, GX)}
    side_dest = [{"gz": lax.rem(side + GZ, GZ)} for side in z_side]
    sends_halo = [has_low, has_high] + has_side
    gets_halo = [has_high, has_low] + has_side
    greet = [low_dest, high_dest] + side_dest

    barrier = pltpu.get_barrier_semaphore()
    for d in range(4):
        @pl.when(sends_halo[d])
        def _(d=d):
            pl.semaphore_signal(barrier, inc=1, device_id=greet[d], device_id_type=MESH)
    count = 0
    for stage in stages[:2]:
        for peer in stage:
            pl.semaphore_signal(barrier, inc=1, device_id=peer, device_id_type=MESH)
            count += 1

    zero_x = jnp.zeros((2, NZ, 8, 128), jnp.float32)
    zero_z = jnp.zeros((NX, 2, 8, 128), jnp.float32)

    @pl.when(gx == 0)
    def _():
        for n in range(7):
            U[n, 0:2, 2 : NZ + 2] = zero_x

    @pl.when(gx == GX - 1)
    def _():
        for n in range(7):
            U[n, NX + 2 : NX + 4, 2 : NZ + 2] = zero_x

    @pl.when(gz == 0)
    def _():
        for n in range(7):
            U[n, 2 : NX + 2, 0:2] = zero_z

    @pl.when(gz == GZ - 1)
    def _():
        for n in range(7):
            U[n, 2 : NX + 2, NZ + 2 : NZ + 4] = zero_z

    def to_tiles(read, write, first=0, planes=NX):
        def plane(x, carry):
            for zt in range(NZ // 8):
                parts = [read(k, x, zt) for k in range(8)]
                write(x, zt * 8, jnp.swapaxes(jnp.stack(parts, axis=0), 0, 1))
            return carry
        lax.fori_loop(first, first + planes, plane, 0)

    def read_wave(slot):
        def read(k, x, zt):
            y = (k % 4) * 128
            return natural[slot, k // 4, x, zt * 8 : zt * 8 + 8, y : y + 128]
        return read

    def read_plain(ref):
        def read(k, x, zt):
            y = (k % 4) * 128
            return ref[x, zt * 8 : zt * 8 + 8, y : y + 128].astype(jnp.float32)
        return read

    def write_now(x, z, tiles):
        U[0, x + 2, z + 2 : z + 10] = tiles

    def write_velocity(x, z, tiles):
        V[x, z : z + 8] = tiles
        C[x, z : z + 8] = courant * tiles * tiles

    def write_prev(x, z, tiles):
        W0[x, z : z + 8] = tiles

    def write_obs(x, z, tiles):
        OB[x, z : z + 8] = tiles

    def write_mask(x, z, tiles):
        MK[x, z : z + 8] = tiles

    def halo(n, s, d):
        field = U.at[n]
        rows = pl.ds(2 + half[s] * ZC, ZC)
        inner = pl.ds(2, NX)
        source, target, dest = [
            ((pl.ds(2, 2), rows), (pl.ds(NX + 2, 2), rows), low_dest),
            ((pl.ds(NX, 2), rows), (pl.ds(0, 2), rows), high_dest),
            (
                (inner, pl.ds(2 + half[s] * (NZ - 2), 2)),
                (inner, pl.ds((1 - half[s]) * (NZ + 2), 2)),
                side_dest[s],
            ),
        ][d]
        return pltpu.make_async_remote_copy(
            src_ref=field.at[source],
            dst_ref=field.at[target],
            send_sem=halo_send.at[n, s * 3 + d],
            recv_sem=halo_recv.at[n, s * 3 + d],
            device_id=dest,
            device_id_type=MESH,
        )

    def send_halo(n, s, d):
        @pl.when(sends_halo[d if d < 2 else 2 + s])
        def _():
            halo(n, s, d).start()

    def wait_halo(n, s, d):
        @pl.when(gets_halo[d if d < 2 else 2 + s])
        def _():
            halo(n, s, d).wait_recv()

    loads[0].wait()
    to_tiles(read_wave(0), write_now, 0, 2)
    to_tiles(read_wave(0), write_now, NX - 2, 2)
    peers = count
    for gets in gets_halo:
        peers = peers + jnp.where(gets, 1, 0)
    pl.semaphore_wait(barrier, peers)
    for s in (0, 1):
        for d in (0, 1):
            send_halo(0, s, d)
    to_tiles(read_wave(0), write_now, 2, NX - 4)
    for s in (0, 1):
        send_halo(0, s, 2)

    loads[1].wait()
    to_tiles(read_wave(1), write_velocity)

    slab = NX // PA
    vel_copies = []
    for j in (1, 2, 3):
        q = lax.rem(pa + j, PA)
        vel_copies.append(
            pltpu.make_async_remote_copy(
                src_ref=V.at[pl.ds(q * slab, slab)],
                dst_ref=RV.at[j],
                send_sem=vel_send.at[j],
                recv_sem=vel_recv.at[j],
                device_id={"pa": q},
                device_id_type=MESH,
            )
        )
    for copy in vel_copies:
        copy.start()

    loads[2].wait()
    to_tiles(read_wave(2), write_prev)
    loads[3].wait()
    to_tiles(read_plain(natural_obs), write_obs)
    loads[4].wait()
    to_tiles(read_plain(natural_rec), write_mask)

    shape = (ZC, 8, 128)
    lane = lax.broadcasted_iota(jnp.int32, shape, 2)
    sub = lax.broadcasted_iota(jnp.int32, shape, 1)
    lane2 = lax.broadcasted_iota(jnp.int32, (8, 128), 1)
    sub2 = lax.broadcasted_iota(jnp.int32, (8, 128), 0)

    scale = (
        jnp.full((8, 128), spread[0], jnp.int32).astype(jnp.float32)
        / jnp.full((8, 128), spread[1], jnp.int32).astype(jnp.float32)
    )
    pull = 2.0 / scale

    def laplace(n, x, z):
        here = U[n, x + 2, pl.ds(z + 2, ZC)]
        near = U[n, x + 1, pl.ds(z + 2, ZC)] + U[n, x + 3, pl.ds(z + 2, ZC)]
        far = U[n, x, pl.ds(z + 2, ZC)] + U[n, x + 4, pl.ds(z + 2, ZC)]
        near = near + (U[n, x + 2, pl.ds(z + 1, ZC)] + U[n, x + 2, pl.ds(z + 3, ZC)])
        far = far + (U[n, x + 2, pl.ds(z, ZC)] + U[n, x + 2, pl.ds(z + 4, ZC)])
        before = pltpu.roll(here, 1, 1)
        before = jnp.where((sub == 0) | (sub == 4), 0.0, before)
        after = pltpu.roll(here, 7, 1)
        after = jnp.where((sub == 3) | (sub == 7), 0.0, after)
        near = near + (
            pltpu.roll(jnp.where(lane == 127, before, here), 1, 2)
            + pltpu.roll(jnp.where(lane == 0, after, here), 127, 2)
        )
        far = far + (
            pltpu.roll(jnp.where(lane >= 126, before, here), 2, 2)
            + pltpu.roll(jnp.where(lane <= 1, after, here), 126, 2)
        )
        return here, centre_coef * here + near_coef * near + far_coef * far

    def advance(n, x, z):
        here, applied = laplace(n, x, z)
        at = (x, pl.ds(z, ZC))
        inner = (x + 2, pl.ds(z + 2, ZC))
        if n < STEPS:
            older = W0[at] if n == 0 else U[(n - 1,) + inner]
            newer = 2.0 * here - older + C[at] * applied
            if n < STEPS - 1:
                L[(n,) + at] = applied
                U[(n + 1,) + inner] = newer
            else:
                adjoint = MK[at] * (newer - OB[at])
                S[at] = adjoint * applied
                LAM[(0,) + at] = adjoint
                U[(n + 1,) + inner] = C[at] * adjoint
        else:
            k = n - STEPS
            adjoint = 2.0 * LAM[(k,) + at] + applied
            if k > 0:
                adjoint = adjoint - LAM[(k - 1,) + at]
            total = S[at] + adjoint * L[(STEPS - 2 - k,) + at]
            if k < STEPS - 2:
                S[at] = total
                LAM[(k + 1,) + at] = adjoint
                U[(n + 1,) + inner] = C[at] * adjoint
            else:
                velocity = V[at]
                H[at] = (2.0 * courant) * velocity * total + pull[None] * (velocity - middle)

    def planes(n, s, first, count_x):
        def body(x, carry):
            advance(n, x, half[s] * ZC)
            return carry
        lax.fori_loop(first, first + count_x, body, 0)

    def ar_copies(stage):
        return [
            pltpu.make_async_remote_copy(
                src_ref=CUR.at[stage],
                dst_ref=AR.at[stage, j],
                send_sem=ar_send.at[stage, j],
                recv_sem=ar_recv.at[stage, j],
                device_id=peer,
                device_id_type=MESH,
            )
            for j, peer in enumerate(stages[stage])
        ]

    def ar_start(stage):
        for copy in ar_copies(stage):
            copy.start()

    def ar_finish(stage):
        total = CUR[stage]
        for j, copy in enumerate(ar_copies(stage)):
            copy.wait_recv()
            total = total + AR[stage, j]
        CUR[stage + 1] = total

    def pair_sums():
        for copy in vel_copies:
            copy.wait_recv()

        def body(i, sums):
            x, z = i // NZ, lax.rem(i, NZ)
            tile = [V[pa * slab + x, z]] + [RV[j, x, z] for j in (1, 2, 3)]
            swapped = [pltpu.roll(t, 4, 0) for t in tile]
            out, at = [], 0
            for a in range(4):
                for b in range(a, 4):
                    if b > a:
                        delta = tile[a] - tile[b]
                        out.append(sums[at] + delta * delta)
                        at += 1
                    delta = tile[a] - swapped[b]
                    out.append(sums[at] + delta * delta)
                    at += 1
            return tuple(out)

        zero = jnp.zeros((8, 128), jnp.float32)
        sums = lax.fori_loop(0, slab * NZ, body, (zero,) * 16)
        groups = [lax.rem(pa + PA - j, PA) for j in range(4)]
        table, at = zero, 0
        for a in range(4):
            for b in range(a, 4):
                if b > a:
                    plain = jnp.sum(sums[at], axis=1, keepdims=True)
                    at += 1
                    spot = (lane2 == groups[a] * 8 + groups[b] * 2) | (lane2 == groups[b] * 8 + groups[a] * 2)
                    table = jnp.where(spot, plain, table)
                crossed = jnp.sum(sums[at], axis=1, keepdims=True)
                at += 1
                table = jnp.where(lane2 == groups[a] * 8 + groups[b] * 2 + 1, crossed, table)
                if b > a:
                    turned = pltpu.roll(jnp.broadcast_to(crossed, (8, 128)), 4, 0)
                    table = jnp.where(lane2 == groups[b] * 8 + groups[a] * 2 + 1, turned, table)
        CUR[0] = table

    firsts = [2, 4, 0, NX - 2]

    def chunk(c):
        return pl.ds(firsts[c % 4], 2), pl.ds(half[c // 4] * ZC, ZC)

    def h_copy(kind, c, src, dest):
        return pltpu.make_async_remote_copy(
            src_ref=src,
            dst_ref=HR.at[kind, c],
            send_sem=h_send.at[kind, c],
            recv_sem=h_recv.at[kind, c],
            device_id={"pa": dest},
            device_id_type=MESH,
        )

    def h_own(c):
        return h_copy(0, c, H.at[chunk(c)], partner)

    def h_across(c):
        return h_copy(1, c, H.at[chunk(c)], across)

    def h_forward(c):
        return h_copy(2, c, HR.at[1, c], partner)

    def h_start(c):
        h_across(c).start()
        h_own(c).start()

    for n in range(7):
        for s in (0, 1):
            wait_halo(n, s, 2)
            planes(n, s, 2, NX - 4)
            if n == 6:
                h_start(4 * s)
                h_start(4 * s + 1)
            wait_halo(n, s, 0)
            wait_halo(n, s, 1)
            planes(n, s, 0, 2)
            if n < 6:
                send_halo(n + 1, s, 0)
            else:
                h_start(4 * s + 2)
            planes(n, s, NX - 2, 2)
            if n < 6:
                send_halo(n + 1, s, 1)
                send_halo(n + 1, s, 2)
            else:
                h_start(4 * s + 3)
        if n == 2:
            pair_sums()
            ar_start(0)
        elif n > 2:
            ar_finish(n - 3)
            ar_start(n - 2)

    chunks = range(8)
    for c in chunks:
        h_across(c).wait_recv()
        h_forward(c).start()
    ar_finish(4)

    table = CUR[5]
    low = jnp.sum(jnp.where(sub2 < 4, table, 0.0), axis=0, keepdims=True)
    high = jnp.sum(jnp.where(sub2 < 4, 0.0, table), axis=0, keepdims=True)
    weight = jnp.exp(-(jnp.where(sub2 < 4, low, high) / cells) / scale)

    def column(index):
        picked = jnp.sum(jnp.where(lane2 == index, weight, 0.0), axis=1, keepdims=True)
        return jnp.broadcast_to(picked, (8, 128))

    groups = [pa, partner, across, diagonal]
    plain = [column(pa * 8 + g * 2) for g in groups]
    crossed = [column(pa * 8 + g * 2 + 1) for g in groups]
    all_weights = plain[0] + crossed[0]
    for g in (1, 2, 3):
        all_weights = all_weights + (plain[g] + crossed[g])
    count_all = 2 * PA
    own = pull * all_weights / count_all
    plain = [-w / count_all for w in plain]
    crossed = [-w / count_all for w in crossed]

    outs = []
    for c in chunks:
        h_own(c).wait_recv()
        h_forward(c).wait_recv()
        x0, z = firsts[c % 4], pl.multiple_of(half[c // 4] * ZC, ZC)
        for i in range(2):
            x = x0 + i
            result = own[None] * (V[x, pl.ds(z, ZC)] - middle)
            for g in range(4):
                tile = H[x, pl.ds(z, ZC)] if g == 0 else HR[g - 1, c, i]
                result = result + plain[g][None] * tile + crossed[g][None] * pltpu.roll(tile, 4, 1)
            result = jnp.swapaxes(result, 0, 1)
            for k in range(8):
                y = (k % 4) * 128
                natural_out[k // 4, x, pl.ds(z, ZC), y : y + 128] = result[k]
        at = (slice(None), pl.ds(x0, 2), pl.ds(z, ZC))
        copy = pltpu.make_async_copy(natural_out.at[at], out_hbm.at[at], out_sem.at[c])
        copy.start()
        outs.append(copy)

    for n in range(7):
        for s in (0, 1):
            for d in range(3):
                @pl.when(sends_halo[d if d < 2 else 2 + s])
                def _(n=n, s=s, d=d):
                    halo(n, s, d).wait_send()
    for copy in vel_copies:
        copy.wait_send()
    for stage in range(5):
        for copy in ar_copies(stage):
            copy.wait_send()
    for c in chunks:
        h_across(c).wait_send()
        h_own(c).wait_send()
        h_forward(c).wait_send()
    for copy in outs:
        copy.wait()


def local(velocity, wave_now, wave_prev, observed, receiver, spread):
    GX, GZ, PA = lax.axis_size("gx"), lax.axis_size("gz"), lax.axis_size("pa")
    particles, NX, NZ, NY = velocity.shape
    cells = float(NX * GX * NZ * GZ * NY)
    any_space = pl.BlockSpec(memory_space=pl.ANY)
    tiles = (NX, NZ, 8, 128)
    f32 = jnp.float32
    dma = pltpu.SemaphoreType.DMA
    return pl.pallas_call(
        functools.partial(kernel, GX, GZ, PA, cells, NX, NZ),
        out_shape=jax.ShapeDtypeStruct(velocity.shape, f32),
        in_specs=[pl.BlockSpec(memory_space=pltpu.SMEM)] + [any_space] * 5,
        out_specs=any_space,
        scratch_shapes=[
            pltpu.VMEM((3,) + velocity.shape, f32),
            pltpu.VMEM(observed.shape, f32),
            pltpu.VMEM(receiver.shape, jnp.int32),
            pltpu.VMEM(velocity.shape, f32),
            pltpu.VMEM((7, NX + 4, NZ + 4, 8, 128), f32),
            pltpu.VMEM(tiles, f32),
            pltpu.VMEM(tiles, f32),
            pltpu.VMEM(tiles, f32),
            pltpu.VMEM((3,) + tiles, f32),
            pltpu.VMEM((3,) + tiles, f32),
            pltpu.VMEM(tiles, f32),
            pltpu.VMEM(tiles, f32),
            pltpu.VMEM(tiles, f32),
            pltpu.VMEM((4, NX // PA, NZ, 8, 128), f32),
            pltpu.VMEM((5, GZ - 1, 8, 128), f32),
            pltpu.VMEM((6, 8, 128), f32),
            pltpu.VMEM(tiles, f32),
            pltpu.VMEM((3, 8, 2, ZC, 8, 128), f32),
            dma((5,)),
            dma((8,)),
            dma((7, 6)),
            dma((7, 6)),
            dma((4,)),
            dma((4,)),
            dma((5, GZ - 1)),
            dma((5, GZ - 1)),
            dma((3, 8)),
            dma((3, 8)),
        ],
        compiler_params=pltpu.CompilerParams(collective_id=0, has_side_effects=True),
    )(spread, velocity, wave_now, wave_prev, observed, receiver)


def solution(mesh):
    in_specs = (
        P("pa", "gx", "gz", None),
        P("pa", "gx", "gz", None),
        P("pa", "gx", "gz", None),
        P("gx", "gz", None),
        P("gx", "gz", None),
        P(),
    )
    out_specs = P("pa", "gx", "gz", None)
    return jax.shard_map(local, mesh=mesh, in_specs=in_specs, out_specs=out_specs, check_vma=False)
```

```python
import functools

import jax
import jax.numpy as jnp
from jax import lax
from jax.experimental import pallas as pl
from jax.experimental.pallas import tpu as pltpu
from jax.sharding import PartitionSpec as P


STEPS = 4
courant = 0.045
centre_coef = -7.5
near_coef = 4.0 / 3.0
far_coef = -1.0 / 12.0
middle = 1.5
ZC = 8
MESH = pl.DeviceIdType.MESH


def kernel(
    GX, GZ, PA, cells, NX, NZ,
    spread, vel_hbm, now_hbm, prev_hbm, obs_hbm, rec_hbm, out_hbm,
    natural, natural_obs, natural_rec, natural_out,
    U, V, C, W0, L, LAM, S, OB, MK,
    RV, AR, CUR, H, HR,
    in_sem, out_sem, halo_send, halo_recv, vel_send, vel_recv, ar_send, ar_recv,
    h_send, h_recv,
):
    gx, gz, pa = lax.axis_index("gx"), lax.axis_index("gz"), lax.axis_index("pa")
    core, hi = lax.rem(pa, 2), pa // 2
    partner = hi * 2 + (1 - core)
    across = (1 - hi) * 2 + core
    diagonal = (1 - hi) * 2 + (1 - core)

    loads = [
        pltpu.make_async_copy(now_hbm, natural.at[0], in_sem.at[0]),
        pltpu.make_async_copy(vel_hbm, natural.at[1], in_sem.at[1]),
        pltpu.make_async_copy(prev_hbm, natural.at[2], in_sem.at[2]),
        pltpu.make_async_copy(obs_hbm, natural_obs, in_sem.at[3]),
        pltpu.make_async_copy(rec_hbm, natural_rec, in_sem.at[4]),
    ]
    for load in loads:
        load.start()

    def turn(index, group, stride, step):
        low = lax.rem(index, stride)
        digit = lax.rem(index // stride, group)
        high = index // (stride * group)
        return (high * group + lax.rem(digit + step, group)) * stride + low

    def flip(index, stride):
        return index + stride * (1 - 2 * lax.rem(index // stride, 2))

    stages = [
        [{"pa": turn(pa, PA, 1, j)} for j in range(1, PA)],
        [{"gz": turn(gz, GZ, 1, j)} for j in range(1, GZ)],
        [{"gx": turn(gx, 4, 1, j)} for j in (1, 2, 3)],
        [{"gx": flip(gx, 4)}],
        [{"gx": flip(gx, 8)}],
    ]
    half = [lax.rem(gz, 2), 1 - lax.rem(gz, 2)]
    z_side = [gz + 2 * h - 1 for h in half]
    has_low, has_high = gx > 0, gx < GX - 1
    has_side = [(side >= 0) & (side < GZ) for side in z_side]
    low_dest = {"gx": lax.rem(gx + GX - 1, GX)}
    high_dest = {"gx": lax.rem(gx + 1, GX)}
    side_dest = [{"gz": lax.rem(side + GZ, GZ)} for side in z_side]
    sends_halo = [has_low, has_high] + has_side
    gets_halo = [has_high, has_low] + has_side
    greet = [low_dest, high_dest] + side_dest

    barrier = pltpu.get_barrier_semaphore()
    for d in range(4):
        @pl.when(sends_halo[d])
        def _(d=d):
            pl.semaphore_signal(barrier, inc=1, device_id=greet[d], device_id_type=MESH)
    count = 0
    for stage in stages[:2]:
        for peer in stage:
            pl.semaphore_signal(barrier, inc=1, device_id=peer, device_id_type=MESH)
            count += 1

    zero_x = jnp.zeros((2, NZ, 8, 128), jnp.float32)
    zero_z = jnp.zeros((NX, 2, 8, 128), jnp.float32)

    @pl.when(gx == 0)
    def _():
        for n in range(7):
            U[n, 0:2, 2 : NZ + 2] = zero_x

    @pl.when(gx == GX - 1)
    def _():
        for n in range(7):
            U[n, NX + 2 : NX + 4, 2 : NZ + 2] = zero_x

    @pl.when(gz == 0)
    def _():
        for n in range(7):
            U[n, 2 : NX + 2, 0:2] = zero_z

    @pl.when(gz == GZ - 1)
    def _():
        for n in range(7):
            U[n, 2 : NX + 2, NZ + 2 : NZ + 4] = zero_z

    def to_tiles(read, write, first=0, planes=NX):
        def plane(x, carry):
            for zt in range(NZ // 8):
                parts = [read(k, x, zt) for k in range(8)]
                write(x, zt * 8, jnp.swapaxes(jnp.stack(parts, axis=0), 0, 1))
            return carry
        lax.fori_loop(first, first + planes, plane, 0)

    def read_wave(slot):
        def read(k, x, zt):
            y = (k % 4) * 128
            return natural[slot, k // 4, x, zt * 8 : zt * 8 + 8, y : y + 128]
        return read

    def read_plain(ref):
        def read(k, x, zt):
            y = (k % 4) * 128
            return ref[x, zt * 8 : zt * 8 + 8, y : y + 128].astype(jnp.float32)
        return read

    def write_now(x, z, tiles):
        U[0, x + 2, z + 2 : z + 10] = tiles

    def write_velocity(x, z, tiles):
        V[x, z : z + 8] = tiles
        C[x, z : z + 8] = courant * tiles * tiles

    def write_prev(x, z, tiles):
        W0[x, z : z + 8] = tiles

    def write_obs(x, z, tiles):
        OB[x, z : z + 8] = tiles

    def write_mask(x, z, tiles):
        MK[x, z : z + 8] = tiles

    def halo(n, s, d):
        field = U.at[n]
        rows = pl.ds(2 + half[s] * ZC, ZC)
        inner = pl.ds(2, NX)
        source, target, dest = [
            ((pl.ds(2, 2), rows), (pl.ds(NX + 2, 2), rows), low_dest),
            ((pl.ds(NX, 2), rows), (pl.ds(0, 2), rows), high_dest),
            (
                (inner, pl.ds(2 + half[s] * (NZ - 2), 2)),
                (inner, pl.ds((1 - half[s]) * (NZ + 2), 2)),
                side_dest[s],
            ),
        ][d]
        return pltpu.make_async_remote_copy(
            src_ref=field.at[source],
            dst_ref=field.at[target],
            send_sem=halo_send.at[n, s * 3 + d],
            recv_sem=halo_recv.at[n, s * 3 + d],
            device_id=dest,
            device_id_type=MESH,
        )

    def send_halo(n, s, d):
        @pl.when(sends_halo[d if d < 2 else 2 + s])
        def _():
            halo(n, s, d).start()

    def wait_halo(n, s, d):
        @pl.when(gets_halo[d if d < 2 else 2 + s])
        def _():
            halo(n, s, d).wait_recv()

    loads[0].wait()
    to_tiles(read_wave(0), write_now, 0, 2)
    to_tiles(read_wave(0), write_now, NX - 2, 2)
    peers = count
    for gets in gets_halo:
        peers = peers + jnp.where(gets, 1, 0)
    pl.semaphore_wait(barrier, peers)
    for s in (0, 1):
        for d in (0, 1):
            send_halo(0, s, d)
    to_tiles(read_wave(0), write_now, 2, NX - 4)
    for s in (0, 1):
        send_halo(0, s, 2)

    loads[1].wait()
    to_tiles(read_wave(1), write_velocity)

    slab = NX // PA
    vel_copies = []
    for j in (1, 2, 3):
        q = lax.rem(pa + j, PA)
        vel_copies.append(
            pltpu.make_async_remote_copy(
                src_ref=V.at[pl.ds(q * slab, slab)],
                dst_ref=RV.at[j],
                send_sem=vel_send.at[j],
                recv_sem=vel_recv.at[j],
                device_id={"pa": q},
                device_id_type=MESH,
            )
        )
    for copy in vel_copies:
        copy.start()

    loads[2].wait()
    to_tiles(read_wave(2), write_prev)
    loads[3].wait()
    to_tiles(read_plain(natural_obs), write_obs)
    loads[4].wait()
    to_tiles(read_plain(natural_rec), write_mask)

    shape = (ZC, 8, 128)
    lane = lax.broadcasted_iota(jnp.int32, shape, 2)
    sub = lax.broadcasted_iota(jnp.int32, shape, 1)
    lane2 = lax.broadcasted_iota(jnp.int32, (8, 128), 1)
    sub2 = lax.broadcasted_iota(jnp.int32, (8, 128), 0)

    scale = (
        jnp.full((8, 128), spread[0], jnp.int32).astype(jnp.float32)
        / jnp.full((8, 128), spread[1], jnp.int32).astype(jnp.float32)
    )
    pull = 2.0 / scale

    def laplace(n, x, z):
        here = U[n, x + 2, pl.ds(z + 2, ZC)]
        near = U[n, x + 1, pl.ds(z + 2, ZC)] + U[n, x + 3, pl.ds(z + 2, ZC)]
        far = U[n, x, pl.ds(z + 2, ZC)] + U[n, x + 4, pl.ds(z + 2, ZC)]
        near = near + (U[n, x + 2, pl.ds(z + 1, ZC)] + U[n, x + 2, pl.ds(z + 3, ZC)])
        far = far + (U[n, x + 2, pl.ds(z, ZC)] + U[n, x + 2, pl.ds(z + 4, ZC)])
        before = pltpu.roll(here, 1, 1)
        before = jnp.where((sub == 0) | (sub == 4), 0.0, before)
        after = pltpu.roll(here, 7, 1)
        after = jnp.where((sub == 3) | (sub == 7), 0.0, after)
        near = near + (
            pltpu.roll(jnp.where(lane == 127, before, here), 1, 2)
            + pltpu.roll(jnp.where(lane == 0, after, here), 127, 2)
        )
        far = far + (
            pltpu.roll(jnp.where(lane >= 126, before, here), 2, 2)
            + pltpu.roll(jnp.where(lane <= 1, after, here), 126, 2)
        )
        return here, centre_coef * here + near_coef * near + far_coef * far

    def advance(n, x, z):
        here, applied = laplace(n, x, z)
        at = (x, pl.ds(z, ZC))
        inner = (x + 2, pl.ds(z + 2, ZC))
        if n < STEPS:
            older = W0[at] if n == 0 else U[(n - 1,) + inner]
            newer = 2.0 * here - older + C[at] * applied
            if n < STEPS - 1:
                L[(n,) + at] = applied
                U[(n + 1,) + inner] = newer
            else:
                adjoint = MK[at] * (newer - OB[at])
                S[at] = adjoint * applied
                LAM[(0,) + at] = adjoint
                U[(n + 1,) + inner] = C[at] * adjoint
        else:
            k = n - STEPS
            adjoint = 2.0 * LAM[(k,) + at] + applied
            if k > 0:
                adjoint = adjoint - LAM[(k - 1,) + at]
            total = S[at] + adjoint * L[(STEPS - 2 - k,) + at]
            if k < STEPS - 2:
                S[at] = total
                LAM[(k + 1,) + at] = adjoint
                U[(n + 1,) + inner] = C[at] * adjoint
            else:
                velocity = V[at]
                H[at] = (2.0 * courant) * velocity * total + pull[None] * (velocity - middle)

    def planes(n, s, first, count_x):
        def body(x, carry):
            advance(n, x, half[s] * ZC)
            return carry
        lax.fori_loop(first, first + count_x, body, 0, unroll=count_x == 2)

    def ar_copies(stage):
        return [
            pltpu.make_async_remote_copy(
                src_ref=CUR.at[stage],
                dst_ref=AR.at[stage, j],
                send_sem=ar_send.at[stage, j],
                recv_sem=ar_recv.at[stage, j],
                device_id=peer,
                device_id_type=MESH,
            )
            for j, peer in enumerate(stages[stage])
        ]

    def ar_start(stage):
        for copy in ar_copies(stage):
            copy.start()

    def ar_finish(stage):
        total = CUR[stage]
        for j, copy in enumerate(ar_copies(stage)):
            copy.wait_recv()
            total = total + AR[stage, j]
        CUR[stage + 1] = total

    def pair_sums():
        for copy in vel_copies:
            copy.wait_recv()

        def body(i, sums):
            x, z = i // NZ, lax.rem(i, NZ)
            tile = [V[pa * slab + x, z]] + [RV[j, x, z] for j in (1, 2, 3)]
            swapped = [pltpu.roll(t, 4, 0) for t in tile]
            out, at = [], 0
            for a in range(4):
                for b in range(a, 4):
                    if b > a:
                        delta = tile[a] - tile[b]
                        out.append(sums[at] + delta * delta)
                        at += 1
                    delta = tile[a] - swapped[b]
                    out.append(sums[at] + delta * delta)
                    at += 1
            return tuple(out)

        zero = jnp.zeros((8, 128), jnp.float32)
        sums = lax.fori_loop(0, slab * NZ, body, (zero,) * 16)
        groups = [lax.rem(pa + PA - j, PA) for j in range(4)]
        table, at = zero, 0
        for a in range(4):
            for b in range(a, 4):
                if b > a:
                    plain = jnp.sum(sums[at], axis=1, keepdims=True)
                    at += 1
                    spot = (lane2 == groups[a] * 8 + groups[b] * 2) | (lane2 == groups[b] * 8 + groups[a] * 2)
                    table = jnp.where(spot, plain, table)
                crossed = jnp.sum(sums[at], axis=1, keepdims=True)
                at += 1
                table = jnp.where(lane2 == groups[a] * 8 + groups[b] * 2 + 1, crossed, table)
                if b > a:
                    turned = pltpu.roll(jnp.broadcast_to(crossed, (8, 128)), 4, 0)
                    table = jnp.where(lane2 == groups[b] * 8 + groups[a] * 2 + 1, turned, table)
        CUR[0] = table

    firsts = [2, 4, 0, NX - 2]

    def chunk(c):
        return pl.ds(firsts[c % 4], 2), pl.ds(half[c // 4] * ZC, ZC)

    def h_copy(kind, c, src, dest):
        return pltpu.make_async_remote_copy(
            src_ref=src,
            dst_ref=HR.at[kind, c],
            send_sem=h_send.at[kind, c],
            recv_sem=h_recv.at[kind, c],
            device_id={"pa": dest},
            device_id_type=MESH,
        )

    def h_own(c):
        return h_copy(0, c, H.at[chunk(c)], partner)

    def h_across(c):
        return h_copy(1, c, H.at[chunk(c)], across)

    def h_forward(c):
        return h_copy(2, c, HR.at[1, c], partner)

    def h_start(c):
        h_across(c).start()
        h_own(c).start()

    for n in range(7):
        for s in (0, 1):
            wait_halo(n, s, 2)
            planes(n, s, 2, NX - 4)
            if n == 6:
                h_start(4 * s)
                h_start(4 * s + 1)
            wait_halo(n, s, 0)
            wait_halo(n, s, 1)
            planes(n, s, 0, 2)
            if n < 6:
                send_halo(n + 1, s, 0)
            else:
                h_start(4 * s + 2)
            planes(n, s, NX - 2, 2)
            if n < 6:
                send_halo(n + 1, s, 1)
                send_halo(n + 1, s, 2)
            else:
                h_start(4 * s + 3)
            if s == 0 and n == 2:
                pair_sums()
                ar_start(0)
            elif s == 0 and n > 2:
                ar_finish(n - 3)
                ar_start(n - 2)

    chunks = range(8)
    for c in chunks:
        h_across(c).wait_recv()
        h_forward(c).start()
    ar_finish(4)

    table = CUR[5]
    low = jnp.sum(jnp.where(sub2 < 4, table, 0.0), axis=0, keepdims=True)
    high = jnp.sum(jnp.where(sub2 < 4, 0.0, table), axis=0, keepdims=True)
    weight = jnp.exp(-(jnp.where(sub2 < 4, low, high) / cells) / scale)

    def column(index):
        picked = jnp.sum(jnp.where(lane2 == index, weight, 0.0), axis=1, keepdims=True)
        return jnp.broadcast_to(picked, (8, 128))

    groups = [pa, partner, across, diagonal]
    plain = [column(pa * 8 + g * 2) for g in groups]
    crossed = [column(pa * 8 + g * 2 + 1) for g in groups]
    all_weights = plain[0] + crossed[0]
    for g in (1, 2, 3):
        all_weights = all_weights + (plain[g] + crossed[g])
    count_all = 2 * PA
    own = pull * all_weights / count_all
    plain = [-w / count_all for w in plain]
    crossed = [-w / count_all for w in crossed]

    outs = []
    for c in chunks:
        h_own(c).wait_recv()
        h_forward(c).wait_recv()
        x0, z = firsts[c % 4], pl.multiple_of(half[c // 4] * ZC, ZC)
        for i in range(2):
            x = x0 + i
            result = own[None] * (V[x, pl.ds(z, ZC)] - middle)
            for g in range(4):
                tile = H[x, pl.ds(z, ZC)] if g == 0 else HR[g - 1, c, i]
                result = result + plain[g][None] * tile + crossed[g][None] * pltpu.roll(tile, 4, 1)
            result = jnp.swapaxes(result, 0, 1)
            for k in range(8):
                y = (k % 4) * 128
                natural_out[k // 4, x, pl.ds(z, ZC), y : y + 128] = result[k]
        at = (slice(None), pl.ds(x0, 2), pl.ds(z, ZC))
        copy = pltpu.make_async_copy(natural_out.at[at], out_hbm.at[at], out_sem.at[c])
        copy.start()
        outs.append(copy)

    for n in range(7):
        for s in (0, 1):
            for d in range(3):
                @pl.when(sends_halo[d if d < 2 else 2 + s])
                def _(n=n, s=s, d=d):
                    halo(n, s, d).wait_send()
    for copy in vel_copies:
        copy.wait_send()
    for stage in range(5):
        for copy in ar_copies(stage):
            copy.wait_send()
    for c in chunks:
        h_across(c).wait_send()
        h_own(c).wait_send()
        h_forward(c).wait_send()
    for copy in outs:
        copy.wait()


def local(velocity, wave_now, wave_prev, observed, receiver, spread):
    GX, GZ, PA = lax.axis_size("gx"), lax.axis_size("gz"), lax.axis_size("pa")
    particles, NX, NZ, NY = velocity.shape
    cells = float(NX * GX * NZ * GZ * NY)
    any_space = pl.BlockSpec(memory_space=pl.ANY)
    tiles = (NX, NZ, 8, 128)
    f32 = jnp.float32
    dma = pltpu.SemaphoreType.DMA
    return pl.pallas_call(
        functools.partial(kernel, GX, GZ, PA, cells, NX, NZ),
        out_shape=jax.ShapeDtypeStruct(velocity.shape, f32),
        in_specs=[pl.BlockSpec(memory_space=pltpu.SMEM)] + [any_space] * 5,
        out_specs=any_space,
        scratch_shapes=[
            pltpu.VMEM((3,) + velocity.shape, f32),
            pltpu.VMEM(observed.shape, f32),
            pltpu.VMEM(receiver.shape, jnp.int32),
            pltpu.VMEM(velocity.shape, f32),
            pltpu.VMEM((7, NX + 4, NZ + 4, 8, 128), f32),
            pltpu.VMEM(tiles, f32),
            pltpu.VMEM(tiles, f32),
            pltpu.VMEM(tiles, f32),
            pltpu.VMEM((3,) + tiles, f32),
            pltpu.VMEM((3,) + tiles, f32),
            pltpu.VMEM(tiles, f32),
            pltpu.VMEM(tiles, f32),
            pltpu.VMEM(tiles, f32),
            pltpu.VMEM((4, NX // PA, NZ, 8, 128), f32),
            pltpu.VMEM((5, GZ - 1, 8, 128), f32),
            pltpu.VMEM((6, 8, 128), f32),
            pltpu.VMEM(tiles, f32),
            pltpu.VMEM((3, 8, 2, ZC, 8, 128), f32),
            dma((5,)),
            dma((8,)),
            dma((7, 6)),
            dma((7, 6)),
            dma((4,)),
            dma((4,)),
            dma((5, GZ - 1)),
            dma((5, GZ - 1)),
            dma((3, 8)),
            dma((3, 8)),
        ],
        compiler_params=pltpu.CompilerParams(collective_id=0, has_side_effects=True),
    )(spread, velocity, wave_now, wave_prev, observed, receiver)


def solution(mesh):
    in_specs = (
        P("pa", "gx", "gz", None),
        P("pa", "gx", "gz", None),
        P("pa", "gx", "gz", None),
        P("gx", "gz", None),
        P("gx", "gz", None),
        P(),
    )
    out_specs = P("pa", "gx", "gz", None)
    return jax.shard_map(local, mesh=mesh, in_specs=in_specs, out_specs=out_specs, check_vma=False)
```

```python
import functools

import jax
import jax.numpy as jnp
from jax import lax
from jax.experimental import pallas as pl
from jax.experimental.pallas import tpu as pltpu
from jax.sharding import PartitionSpec as P


STEPS = 4
courant = 0.045
centre_coef = -7.5
near_coef = 4.0 / 3.0
far_coef = -1.0 / 12.0
middle = 1.5
ZC = 8
MESH = pl.DeviceIdType.MESH


def kernel(
    GX, GZ, PA, cells, NX, NZ,
    spread, vel_hbm, now_hbm, prev_hbm, obs_hbm, rec_hbm, out_hbm,
    natural, natural_obs, natural_rec, natural_out,
    U, V, C, W0, L, LAM, S, OB, MK,
    RV, AR, CUR, H, HR,
    in_sem, out_sem, halo_send, halo_recv, vel_send, vel_recv, ar_send, ar_recv,
    h_send, h_recv,
):
    gx, gz, pa = lax.axis_index("gx"), lax.axis_index("gz"), lax.axis_index("pa")
    core, hi = lax.rem(pa, 2), pa // 2
    partner = hi * 2 + (1 - core)
    across = (1 - hi) * 2 + core
    diagonal = (1 - hi) * 2 + (1 - core)

    loads = [
        pltpu.make_async_copy(now_hbm, natural.at[0], in_sem.at[0]),
        pltpu.make_async_copy(vel_hbm, natural.at[1], in_sem.at[1]),
        pltpu.make_async_copy(prev_hbm, natural.at[2], in_sem.at[2]),
        pltpu.make_async_copy(obs_hbm, natural_obs, in_sem.at[3]),
        pltpu.make_async_copy(rec_hbm, natural_rec, in_sem.at[4]),
    ]
    for load in loads:
        load.start()

    def turn(index, group, stride, step):
        low = lax.rem(index, stride)
        digit = lax.rem(index // stride, group)
        high = index // (stride * group)
        return (high * group + lax.rem(digit + step, group)) * stride + low

    def flip(index, stride):
        return index + stride * (1 - 2 * lax.rem(index // stride, 2))

    stages = [
        [{"pa": turn(pa, PA, 1, j)} for j in range(1, PA)],
        [{"gz": turn(gz, GZ, 1, j)} for j in range(1, GZ)],
        [{"gx": turn(gx, 4, 1, j)} for j in (1, 2, 3)],
        [{"gx": flip(gx, 4)}],
        [{"gx": flip(gx, 8)}],
    ]
    half = [lax.rem(gz, 2), 1 - lax.rem(gz, 2)]
    z_side = [gz + 2 * h - 1 for h in half]
    has_low, has_high = gx > 0, gx < GX - 1
    has_side = [(side >= 0) & (side < GZ) for side in z_side]
    low_dest = {"gx": lax.rem(gx + GX - 1, GX)}
    high_dest = {"gx": lax.rem(gx + 1, GX)}
    side_dest = [{"gz": lax.rem(side + GZ, GZ)} for side in z_side]
    sends_halo = [has_low, has_high] + has_side
    gets_halo = [has_high, has_low] + has_side
    greet = [low_dest, high_dest] + side_dest

    barrier = pltpu.get_barrier_semaphore()
    for d in range(4):
        @pl.when(sends_halo[d])
        def _(d=d):
            pl.semaphore_signal(barrier, inc=1, device_id=greet[d], device_id_type=MESH)
    count = 0
    for stage in stages[:2]:
        for peer in stage:
            pl.semaphore_signal(barrier, inc=1, device_id=peer, device_id_type=MESH)
            count += 1

    zero_x = jnp.zeros((2, NZ, 8, 128), jnp.float32)
    zero_z = jnp.zeros((NX, 2, 8, 128), jnp.float32)

    @pl.when(gx == 0)
    def _():
        for n in range(7):
            U[n, 0:2, 2 : NZ + 2] = zero_x

    @pl.when(gx == GX - 1)
    def _():
        for n in range(7):
            U[n, NX + 2 : NX + 4, 2 : NZ + 2] = zero_x

    @pl.when(gz == 0)
    def _():
        for n in range(7):
            U[n, 2 : NX + 2, 0:2] = zero_z

    @pl.when(gz == GZ - 1)
    def _():
        for n in range(7):
            U[n, 2 : NX + 2, NZ + 2 : NZ + 4] = zero_z

    def to_tiles(read, write, first=0, planes=NX):
        def plane(x, carry):
            for zt in range(NZ // 8):
                parts = [read(k, x, zt) for k in range(8)]
                write(x, zt * 8, jnp.swapaxes(jnp.stack(parts, axis=0), 0, 1))
            return carry
        lax.fori_loop(first, first + planes, plane, 0)

    def read_wave(slot):
        def read(k, x, zt):
            y = (k % 4) * 128
            return natural[slot, k // 4, x, zt * 8 : zt * 8 + 8, y : y + 128]
        return read

    def read_plain(ref):
        def read(k, x, zt):
            y = (k % 4) * 128
            return ref[x, zt * 8 : zt * 8 + 8, y : y + 128].astype(jnp.float32)
        return read

    def write_now(x, z, tiles):
        U[0, x + 2, z + 2 : z + 10] = tiles

    def write_velocity(x, z, tiles):
        V[x, z : z + 8] = tiles
        C[x, z : z + 8] = courant * tiles * tiles

    def write_prev(x, z, tiles):
        W0[x, z : z + 8] = tiles

    def write_obs(x, z, tiles):
        OB[x, z : z + 8] = tiles

    def write_mask(x, z, tiles):
        MK[x, z : z + 8] = tiles

    def halo(n, s, d):
        field = U.at[n]
        rows = pl.ds(2 + half[s] * ZC, ZC)
        inner = pl.ds(2, NX)
        source, target, dest = [
            ((pl.ds(2, 2), rows), (pl.ds(NX + 2, 2), rows), low_dest),
            ((pl.ds(NX, 2), rows), (pl.ds(0, 2), rows), high_dest),
            (
                (inner, pl.ds(2 + half[s] * (NZ - 2), 2)),
                (inner, pl.ds((1 - half[s]) * (NZ + 2), 2)),
                side_dest[s],
            ),
        ][d]
        return pltpu.make_async_remote_copy(
            src_ref=field.at[source],
            dst_ref=field.at[target],
            send_sem=halo_send.at[n, s * 3 + d],
            recv_sem=halo_recv.at[n, s * 3 + d],
            device_id=dest,
            device_id_type=MESH,
        )

    def send_halo(n, s, d):
        @pl.when(sends_halo[d if d < 2 else 2 + s])
        def _():
            halo(n, s, d).start()

    def wait_halo(n, s, d):
        @pl.when(gets_halo[d if d < 2 else 2 + s])
        def _():
            halo(n, s, d).wait_recv()

    loads[0].wait()
    to_tiles(read_wave(0), write_now, 0, 2)
    to_tiles(read_wave(0), write_now, NX - 2, 2)
    peers = count
    for gets in gets_halo:
        peers = peers + jnp.where(gets, 1, 0)
    pl.semaphore_wait(barrier, peers)
    for s in (0, 1):
        for d in (0, 1):
            send_halo(0, s, d)
    to_tiles(read_wave(0), write_now, 2, NX - 4)
    for s in (0, 1):
        send_halo(0, s, 2)

    loads[1].wait()
    to_tiles(read_wave(1), write_velocity)

    slab = NX // PA
    vel_copies = []
    for j in (1, 2, 3):
        q = lax.rem(pa + j, PA)
        vel_copies.append(
            pltpu.make_async_remote_copy(
                src_ref=V.at[pl.ds(q * slab, slab)],
                dst_ref=RV.at[j],
                send_sem=vel_send.at[j],
                recv_sem=vel_recv.at[j],
                device_id={"pa": q},
                device_id_type=MESH,
            )
        )
    for copy in vel_copies:
        copy.start()

    loads[2].wait()
    to_tiles(read_wave(2), write_prev)
    loads[3].wait()
    to_tiles(read_plain(natural_obs), write_obs)
    loads[4].wait()
    to_tiles(read_plain(natural_rec), write_mask)

    shape = (ZC, 8, 128)
    lane = lax.broadcasted_iota(jnp.int32, shape, 2)
    sub = lax.broadcasted_iota(jnp.int32, shape, 1)
    lane2 = lax.broadcasted_iota(jnp.int32, (8, 128), 1)
    sub2 = lax.broadcasted_iota(jnp.int32, (8, 128), 0)

    scale = (
        jnp.full((8, 128), spread[0], jnp.int32).astype(jnp.float32)
        / jnp.full((8, 128), spread[1], jnp.int32).astype(jnp.float32)
    )
    pull = 2.0 / scale

    def laplace(n, x, z):
        here = U[n, x + 2, pl.ds(z + 2, ZC)]
        near = U[n, x + 1, pl.ds(z + 2, ZC)] + U[n, x + 3, pl.ds(z + 2, ZC)]
        far = U[n, x, pl.ds(z + 2, ZC)] + U[n, x + 4, pl.ds(z + 2, ZC)]
        near = near + (U[n, x + 2, pl.ds(z + 1, ZC)] + U[n, x + 2, pl.ds(z + 3, ZC)])
        far = far + (U[n, x + 2, pl.ds(z, ZC)] + U[n, x + 2, pl.ds(z + 4, ZC)])
        before = pltpu.roll(here, 1, 1)
        before = jnp.where((sub == 0) | (sub == 4), 0.0, before)
        after = pltpu.roll(here, 7, 1)
        after = jnp.where((sub == 3) | (sub == 7), 0.0, after)
        near = near + (
            pltpu.roll(jnp.where(lane == 127, before, here), 1, 2)
            + pltpu.roll(jnp.where(lane == 0, after, here), 127, 2)
        )
        far = far + (
            pltpu.roll(jnp.where(lane >= 126, before, here), 2, 2)
            + pltpu.roll(jnp.where(lane <= 1, after, here), 126, 2)
        )
        return here, centre_coef * here + near_coef * near + far_coef * far

    def advance(n, x, z):
        here, applied = laplace(n, x, z)
        at = (x, pl.ds(z, ZC))
        inner = (x + 2, pl.ds(z + 2, ZC))
        if n < STEPS:
            older = W0[at] if n == 0 else U[(n - 1,) + inner]
            newer = 2.0 * here - older + C[at] * applied
            if n < STEPS - 1:
                L[(n,) + at] = applied
                U[(n + 1,) + inner] = newer
            else:
                adjoint = MK[at] * (newer - OB[at])
                S[at] = adjoint * applied
                LAM[(0,) + at] = adjoint
                U[(n + 1,) + inner] = C[at] * adjoint
        else:
            k = n - STEPS
            adjoint = 2.0 * LAM[(k,) + at] + applied
            if k > 0:
                adjoint = adjoint - LAM[(k - 1,) + at]
            total = S[at] + adjoint * L[(STEPS - 2 - k,) + at]
            if k < STEPS - 2:
                S[at] = total
                LAM[(k + 1,) + at] = adjoint
                U[(n + 1,) + inner] = C[at] * adjoint
            else:
                velocity = V[at]
                H[at] = (2.0 * courant) * velocity * total + pull[None] * (velocity - middle)

    def planes(n, s, first, count_x):
        def body(x, carry):
            advance(n, x, half[s] * ZC)
            return carry
        lax.fori_loop(first, first + count_x, body, 0, unroll=count_x == 2)

    def ar_copies(stage):
        return [
            pltpu.make_async_remote_copy(
                src_ref=CUR.at[stage],
                dst_ref=AR.at[stage, j],
                send_sem=ar_send.at[stage, j],
                recv_sem=ar_recv.at[stage, j],
                device_id=peer,
                device_id_type=MESH,
            )
            for j, peer in enumerate(stages[stage])
        ]

    def ar_start(stage):
        for copy in ar_copies(stage):
            copy.start()

    def ar_finish(stage):
        total = CUR[stage]
        for j, copy in enumerate(ar_copies(stage)):
            copy.wait_recv()
            total = total + AR[stage, j]
        CUR[stage + 1] = total

    def pair_sums():
        for copy in vel_copies:
            copy.wait_recv()

        def body(i, sums):
            x, z = i // NZ, lax.rem(i, NZ)
            tile = [V[pa * slab + x, z]] + [RV[j, x, z] for j in (1, 2, 3)]
            swapped = [pltpu.roll(t, 4, 0) for t in tile]
            out, at = [], 0
            for a in range(4):
                for b in range(a, 4):
                    if b > a:
                        delta = tile[a] - tile[b]
                        out.append(sums[at] + delta * delta)
                        at += 1
                    delta = tile[a] - swapped[b]
                    out.append(sums[at] + delta * delta)
                    at += 1
            return tuple(out)

        zero = jnp.zeros((8, 128), jnp.float32)
        sums = lax.fori_loop(0, slab * NZ, body, (zero,) * 16)
        groups = [lax.rem(pa + PA - j, PA) for j in range(4)]
        table, at = zero, 0
        for a in range(4):
            for b in range(a, 4):
                if b > a:
                    plain = jnp.sum(sums[at], axis=1, keepdims=True)
                    at += 1
                    spot = (lane2 == groups[a] * 8 + groups[b] * 2) | (lane2 == groups[b] * 8 + groups[a] * 2)
                    table = jnp.where(spot, plain, table)
                crossed = jnp.sum(sums[at], axis=1, keepdims=True)
                at += 1
                table = jnp.where(lane2 == groups[a] * 8 + groups[b] * 2 + 1, crossed, table)
                if b > a:
                    turned = pltpu.roll(jnp.broadcast_to(crossed, (8, 128)), 4, 0)
                    table = jnp.where(lane2 == groups[b] * 8 + groups[a] * 2 + 1, turned, table)
        CUR[0] = table

    firsts = [2, 4, 0, NX - 2]

    def chunk(c):
        return pl.ds(firsts[c % 4], 2), pl.ds(half[c // 4] * ZC, ZC)

    def h_copy(kind, c, src, dest):
        return pltpu.make_async_remote_copy(
            src_ref=src,
            dst_ref=HR.at[kind, c],
            send_sem=h_send.at[kind, c],
            recv_sem=h_recv.at[kind, c],
            device_id={"pa": dest},
            device_id_type=MESH,
        )

    def h_own(c):
        return h_copy(0, c, H.at[chunk(c)], partner)

    def h_across(c):
        return h_copy(1, c, H.at[chunk(c)], across)

    def h_forward(c):
        return h_copy(2, c, HR.at[1, c], partner)

    def h_start(c):
        h_across(c).start()
        h_own(c).start()

    for n in range(7):
        for s in (0, 1):
            wait_halo(n, s, 2)
            planes(n, s, 2, NX - 4)
            if n == 6:
                h_start(4 * s)
                h_start(4 * s + 1)
            wait_halo(n, s, 0)
            wait_halo(n, s, 1)
            planes(n, s, 0, 2)
            if n < 6:
                send_halo(n + 1, s, 0)
            else:
                h_start(4 * s + 2)
            planes(n, s, NX - 2, 2)
            if n < 6:
                send_halo(n + 1, s, 1)
                send_halo(n + 1, s, 2)
            else:
                h_start(4 * s + 3)
            if s == 0 and n == 2:
                pair_sums()
                ar_start(0)
            elif s == 0 and n > 2:
                ar_finish(n - 3)
                ar_start(n - 2)

    chunks = range(8)

    def forward(c):
        h_across(c).wait_recv()
        h_forward(c).start()

    for c in range(6):
        forward(c)
    ar_finish(4)

    table = CUR[5]
    low = jnp.sum(jnp.where(sub2 < 4, table, 0.0), axis=0, keepdims=True)
    high = jnp.sum(jnp.where(sub2 < 4, 0.0, table), axis=0, keepdims=True)
    weight = jnp.exp(-(jnp.where(sub2 < 4, low, high) / cells) / scale)

    def column(index):
        picked = jnp.sum(jnp.where(lane2 == index, weight, 0.0), axis=1, keepdims=True)
        return jnp.broadcast_to(picked, (8, 128))

    groups = [pa, partner, across, diagonal]
    plain = [column(pa * 8 + g * 2) for g in groups]
    crossed = [column(pa * 8 + g * 2 + 1) for g in groups]
    all_weights = plain[0] + crossed[0]
    for g in (1, 2, 3):
        all_weights = all_weights + (plain[g] + crossed[g])
    count_all = 2 * PA
    own = pull * all_weights / count_all
    plain = [-w / count_all for w in plain]
    crossed = [-w / count_all for w in crossed]

    outs = []

    def combine(c):
        h_own(c).wait_recv()
        h_forward(c).wait_recv()
        x0, z = firsts[c % 4], pl.multiple_of(half[c // 4] * ZC, ZC)
        for i in range(2):
            x = x0 + i
            result = own[None] * (V[x, pl.ds(z, ZC)] - middle)
            for g in range(4):
                tile = H[x, pl.ds(z, ZC)] if g == 0 else HR[g - 1, c, i]
                result = result + plain[g][None] * tile + crossed[g][None] * pltpu.roll(tile, 4, 1)
            result = jnp.swapaxes(result, 0, 1)
            for k in range(8):
                y = (k % 4) * 128
                natural_out[k // 4, x, pl.ds(z, ZC), y : y + 128] = result[k]
        at = (slice(None), pl.ds(x0, 2), pl.ds(z, ZC))
        copy = pltpu.make_async_copy(natural_out.at[at], out_hbm.at[at], out_sem.at[c])
        copy.start()
        outs.append(copy)

    for c in (0, 1):
        combine(c)
    forward(6)
    combine(2)
    forward(7)
    for c in range(3, 8):
        combine(c)

    for n in range(7):
        for s in (0, 1):
            for d in range(3):
                @pl.when(sends_halo[d if d < 2 else 2 + s])
                def _(n=n, s=s, d=d):
                    halo(n, s, d).wait_send()
    for copy in vel_copies:
        copy.wait_send()
    for stage in range(5):
        for copy in ar_copies(stage):
            copy.wait_send()
    for c in chunks:
        h_across(c).wait_send()
        h_own(c).wait_send()
        h_forward(c).wait_send()
    for copy in outs:
        copy.wait()


def local(velocity, wave_now, wave_prev, observed, receiver, spread):
    GX, GZ, PA = lax.axis_size("gx"), lax.axis_size("gz"), lax.axis_size("pa")
    particles, NX, NZ, NY = velocity.shape
    cells = float(NX * GX * NZ * GZ * NY)
    any_space = pl.BlockSpec(memory_space=pl.ANY)
    tiles = (NX, NZ, 8, 128)
    f32 = jnp.float32
    dma = pltpu.SemaphoreType.DMA
    return pl.pallas_call(
        functools.partial(kernel, GX, GZ, PA, cells, NX, NZ),
        out_shape=jax.ShapeDtypeStruct(velocity.shape, f32),
        in_specs=[pl.BlockSpec(memory_space=pltpu.SMEM)] + [any_space] * 5,
        out_specs=any_space,
        scratch_shapes=[
            pltpu.VMEM((3,) + velocity.shape, f32),
            pltpu.VMEM(observed.shape, f32),
            pltpu.VMEM(receiver.shape, jnp.int32),
            pltpu.VMEM(velocity.shape, f32),
            pltpu.VMEM((7, NX + 4, NZ + 4, 8, 128), f32),
            pltpu.VMEM(tiles, f32),
            pltpu.VMEM(tiles, f32),
            pltpu.VMEM(tiles, f32),
            pltpu.VMEM((3,) + tiles, f32),
            pltpu.VMEM((3,) + tiles, f32),
            pltpu.VMEM(tiles, f32),
            pltpu.VMEM(tiles, f32),
            pltpu.VMEM(tiles, f32),
            pltpu.VMEM((4, NX // PA, NZ, 8, 128), f32),
            pltpu.VMEM((5, GZ - 1, 8, 128), f32),
            pltpu.VMEM((6, 8, 128), f32),
            pltpu.VMEM(tiles, f32),
            pltpu.VMEM((3, 8, 2, ZC, 8, 128), f32),
            dma((5,)),
            dma((8,)),
            dma((7, 6)),
            dma((7, 6)),
            dma((4,)),
            dma((4,)),
            dma((5, GZ - 1)),
            dma((5, GZ - 1)),
            dma((3, 8)),
            dma((3, 8)),
        ],
        compiler_params=pltpu.CompilerParams(collective_id=0, has_side_effects=True),
    )(spread, velocity, wave_now, wave_prev, observed, receiver)


def solution(mesh):
    in_specs = (
        P("pa", "gx", "gz", None),
        P("pa", "gx", "gz", None),
        P("pa", "gx", "gz", None),
        P("gx", "gz", None),
        P("gx", "gz", None),
        P(),
    )
    out_specs = P("pa", "gx", "gz", None)
    return jax.shard_map(local, mesh=mesh, in_specs=in_specs, out_specs=out_specs, check_vma=False)
```
